512 devices in a mesh: pa: 8 (over y), pb: 64 (over z, x, core).
Axes of the slice: x: 4, y: 8, z: 8, core: 2. Of those that a mesh axis runs over, the one named last changes fastest.
Arguments:
- matrix: bfloat16 [12288, 24576], P('pa', 'pb'), may hold values from -6 to 6
- panels: bfloat16 [6, 12288, 128], P(None, ('pa', 'pb')), may hold values from -0.25 to 0.25
- inverses: float32 [6, 128, 128], replicated, as said below
- pivots: int32 [6, 128], replicated, may hold values from 128 to 12287, as said below
Outputs:
- factored: bfloat16 [12288, 24576], P('pa', 'pb')
The draws below stay inside these ranges and needn't reach their ends.
Inputs may be any that keep to these rules, and one draw needn't show every extreme that they name: `pivots`: row k lists 128 different row numbers, each at least (k + 1) * 128. `inverses`: each block is unit lower triangular.
All inputs are finite; a program needn't handle non-finite values.
Results may differ from the reference program's by a relative error of at most 0.0082.
Values may be sent and summed in bfloat16 or wider, within the bound.
No kernel may reach another device: no remote copies, remote signals or barrier semaphores. Data moves between devices by JAX's collectives and lax.ppermute only.
A program may use at most 64 MiB of HBM per device.

```python
import jax
import jax.numpy as jnp
from jax import lax

NB = 128
STEPS = 6
C_DEV = 384
ROWS = 12288
COLUMNS = 24576
N_PB = 64


def draw_inverses(key, part):
    noise = jax.random.normal(key, (STEPS, NB, NB), jnp.float32) * 0.05
    strict = jnp.tril(noise, -1)
    return strict + jnp.eye(NB, dtype=jnp.float32)[None, :, :]


def draw_pivots(key, part):
    chosen = []
    for step in range(STEPS):
        low = (step + 1) * NB
        span = ROWS - low
        inner = jax.random.permutation(jax.random.fold_in(key, 2 * step), span - 2)[:NB - 2] + 1
        values = jnp.concatenate([jnp.zeros((1,), jnp.int32), inner.astype(jnp.int32), jnp.full((1,), span - 1, jnp.int32)])
        order = jax.random.permutation(jax.random.fold_in(key, 2 * step + 1), NB)
        chosen.append(jnp.take(values, order) + low)
    return jnp.stack(chosen).astype(jnp.int32)


def block_scale(own_key, extent, shards, smallest, largest):
    loudness, own = 1.0, jax.random.fold_in(own_key, 6)
    for dim, blocks in shards:
        heights = jnp.exp(jax.random.uniform(jax.random.fold_in(own, dim), (blocks,), jnp.float32, smallest / len(shards), largest / len(shards)))
        loudness = loudness * jnp.repeat(heights, extent[dim] // blocks).reshape([-1 if axis == dim else 1 for axis in range(len(extent))])
    return loudness


def normal_values(stream_key, extent, deviation, bound, shards=(), held_as=jnp.bfloat16):
    factor_of = block_scale(stream_key, extent, shards, -0.22, 0.18) if shards else 1.0
    values = jax.random.normal(stream_key, extent, jnp.float32) * deviation * factor_of
    return jnp.minimum(jnp.maximum(values, -bound), bound).astype(held_as)


def setup_inputs(seed: int = 0) -> dict:
    key_of = jax.random.split(jax.random.key(seed), 5)
    return {
        "matrix": normal_values(key_of[0], (ROWS, COLUMNS), 1.0, 6.0, ((0, 8), (1, 64))),
        "panels": normal_values(key_of[1], (STEPS, ROWS, NB), (4 * NB) ** -0.5, 0.25, ((1, 512),)),
        "inverses": draw_inverses(jax.random.fold_in(key_of[4], 71), 0),
        "pivots": draw_pivots(jax.random.fold_in(key_of[4], 71), 0),
    }


def reference(matrix, panels, inverses, pivots):
    total_rows = matrix.shape[0]
    blocks = matrix.reshape(total_rows, N_PB, C_DEV).transpose(1, 0, 2)
    row_ids = jnp.arange(total_rows, dtype=jnp.int32)

    def one_block(block):
        for step in range(STEPS):
            lo = step * NB
            hi = lo + NB
            chosen = pivots[step]
            old_top = block[lo:hi]
            new_top = jnp.take(block, chosen, axis=0)
            block = block.at[chosen].set(old_top)
            block = block.at[lo:hi].set(new_top)
            upper = jnp.dot(inverses[step], new_top.astype(jnp.float32), precision=lax.Precision.HIGHEST, preferred_element_type=jnp.float32).astype(jnp.bfloat16)
            product = jnp.dot(panels[step], upper, preferred_element_type=jnp.float32)
            updated = (block.astype(jnp.float32) - product).astype(jnp.bfloat16)
            block = jnp.where((row_ids >= hi)[:, None], updated, block)
            block = block.at[lo:hi].set(upper)
        return block

    result = lax.map(one_block, blocks)
    return result.transpose(1, 0, 2).reshape(total_rows, N_PB * C_DEV)
```

```python
import functools

import jax
import jax.numpy as jnp
from jax import lax
from jax.experimental import pallas as pl
from jax.experimental.pallas import tpu as pltpu
from jax.sharding import Mesh
from jax.sharding import PartitionSpec as P

NB = 128
STEPS = 6
TOP = NB * STEPS
PAIRS = [(k, j) for k in range(1, STEPS) for j in range(k)]
CHUNK = 64
BF = jnp.bfloat16
F32 = jnp.float32
VM = pl.BlockSpec(memory_space=pltpu.VMEM)
SM = pl.BlockSpec(memory_space=pltpu.SMEM)
ANY = pl.BlockSpec(memory_space=pl.ANY)


def start_of(k):
    return 2 * NB * (k * (k - 1) // 2)


def iota(shape, dim):
    return lax.broadcasted_iota(jnp.int32, shape, dim)


def prep_kernel(first_ref, rows_ref, cols_ref, matrix_ref, picked_ref, tops_ref, select_ref):
    first = first_ref[0]
    ones = jnp.ones((NB, NB), BF)
    local = matrix_ref.shape[0]
    for k in range(STEPS):
        ids = jnp.concatenate([iota((NB, NB), 0) + k * NB, jnp.broadcast_to(cols_ref[k * NB:(k + 1) * NB, :], (NB, NB))])
        found = jnp.zeros((2 * NB, NB), F32)
        for j in reversed(range(k)):
            at = start_of(k) + 2 * NB * j
            same = jnp.where(ids == rows_ref[j:j + 1, :], 1.0, 0.0).astype(F32)
            live = 1.0 - found
            select_ref[:, at:at + NB] = (same * live).astype(BF)
            select_ref[:, at + NB:at + 2 * NB] = (-live).astype(BF)
            hit = jnp.dot(same.astype(BF), ones, preferred_element_type=F32)
            found = jnp.maximum(found, hit)
        fresh = found < 0.5
        where = cols_ref[k * NB:(k + 1) * NB, :] - first
        hot = jnp.where(iota((NB, local), 1) == where, 1.0, 0.0).astype(BF)
        row = jnp.dot(hot, matrix_ref[...], preferred_element_type=F32)
        for c in range(0, row.shape[1], NB):
            picked_ref[k * NB:(k + 1) * NB, c:c + NB] = jnp.where(fresh[NB:], row[:, c:c + NB], 0.0).astype(BF)
            mine = fresh[:NB] & (iota((NB, NB), 0) + first < TOP)
            top = matrix_ref[k * NB:(k + 1) * NB, c:c + NB].astype(F32)
            tops_ref[k * NB:(k + 1) * NB, c:c + NB] = jnp.where(mine, top, 0.0).astype(BF)


def rows_kernel(first_ref, rows_ref, panels_ref, matrix_ref, factor_ref, kept_ref):
    ones = jnp.ones((NB, NB), BF)
    height = 2 * NB

    def one(step, carry):
        at = pl.multiple_of(step * height, height)
        ids = iota((height, NB), 0) + first_ref[0] + at
        is_top = ids < TOP
        found = jnp.zeros((height, NB), F32)
        for j in reversed(range(STEPS)):
            same = jnp.where((ids == rows_ref[j:j + 1, :]) & ~is_top, 1.0, 0.0).astype(F32)
            live = 1.0 - found
            factor_ref[pl.ds(at, height), 2 * NB * j:2 * NB * j + NB] = (same * live).astype(BF)
            diag = jnp.where(ids - NB * j == iota((height, NB), 1), 1.0, 0.0).astype(F32)
            lower = -live * panels_ref[j, pl.ds(at, height), :].astype(F32)
            factor_ref[pl.ds(at, height), 2 * NB * j + NB:2 * NB * (j + 1)] = jnp.where(is_top, diag, lower).astype(BF)
            hit = jnp.dot(same.astype(BF), ones, preferred_element_type=F32)
            found = jnp.maximum(found, hit)
        fresh = (found < 0.5) & ~is_top
        for c in range(0, matrix_ref.shape[1], NB):
            old = matrix_ref[pl.ds(at, height), c:c + NB].astype(F32)
            kept_ref[pl.ds(at, height), c:c + NB] = jnp.where(fresh, old, 0.0).astype(BF)
        return carry

    lax.fori_loop(0, matrix_ref.shape[0] // height, one, 0)


def solve_kernel(core_ref, content_ref, mine_ref, other_ref, inverses_ref, select_ref, factor_hbm, kept_hbm, out_ref,
                 low, coef, state, factor, kept, sems):
    loads = [pltpu.make_async_copy(factor_hbm, factor, sems.at[0]), pltpu.make_async_copy(kept_hbm, kept, sems.at[1])]
    for load in loads:
        load.start()
    half = low.shape[1]
    core = core_ref[0]
    low[core] = mine_ref[...].reshape(half, NB)
    low[1 - core] = other_ref[...].reshape(half, NB)
    parts, each = content_ref.shape[0], content_ref.shape[1] // 2
    width = content_ref.shape[2]
    picked, tops = [], []
    contents = content_ref[:, :each, :].reshape(parts * each, width)
    displaced = content_ref[:, each:, :].reshape(parts * each, width)
    for k in range(STEPS):
        x = jnp.concatenate([displaced[k * NB:(k + 1) * NB], contents[k * NB:(k + 1) * NB]]).astype(F32)
        if k:
            for j in range(k):
                at = start_of(k) + 2 * NB * j
                t = 2 * PAIRS.index((k, j))
                b0, b1 = t * NB, (t + 1) * NB
                block = jnp.concatenate([low[b1 // half, b1 % half:b1 % half + NB, :], low[b0 // half, b0 % half:b0 % half + NB, :]])
                coef[:, 2 * NB * j:2 * NB * j + NB] = select_ref[:, at:at + NB]
                coef[:, 2 * NB * j + NB:2 * NB * (j + 1)] = select_ref[:, at + NB:at + 2 * NB] * block
            x = x + jnp.dot(coef[:, :2 * NB * k], state[:2 * NB * k, :], preferred_element_type=F32)
        y = x.astype(BF)
        state[2 * NB * k:2 * NB * k + NB, :] = y[:NB]
        inv = inverses_ref[k]
        hi = inv.astype(BF)
        rest = inv - hi.astype(F32)
        mid = rest.astype(BF)
        lo = (rest - mid.astype(F32)).astype(BF)
        v = y[NB:]
        upper = jnp.dot(hi, v, preferred_element_type=F32) + (
            jnp.dot(mid, v, preferred_element_type=F32) + jnp.dot(lo, v, preferred_element_type=F32))
        state[2 * NB * k + NB:2 * NB * (k + 1), :] = upper.astype(BF)
    for load in loads:
        load.wait()

    def one(step, carry):
        at = pl.multiple_of(step * 2 * NB, 2 * NB)
        new = jnp.dot(factor[pl.ds(at, 2 * NB), :], state[...], preferred_element_type=F32)
        out_ref[pl.ds(at, 2 * NB), :] = (kept[pl.ds(at, 2 * NB), :].astype(F32) + new).astype(BF)
        return carry

    lax.fori_loop(0, out_ref.shape[0] // (2 * NB), one, 0)


def cost(flops, nbytes):
    return pl.CostEstimate(flops=flops, bytes_accessed=nbytes, transcendentals=0)


def spread(x, axes, parts):
    return lax.all_to_all(jnp.broadcast_to(x[None], (parts,) + x.shape), axes, 0, 0, tiled=True)


def per_device(ny, nzx, nc, matrix, panels, inverses, pivots):
    local, width = matrix.shape
    held = panels.shape[1]
    y, core = lax.axis_index("y"), lax.axis_index("c")
    zx = lax.axis_index(("z", "x"))
    first = y * local
    swap = [(0, 1), (1, 0)]
    first1 = first.reshape(1).astype(jnp.int32)
    core1 = core.reshape(1).astype(jnp.int32)

    mine = spread(panels.reshape(STEPS * held, NB), ("z", "x"), nzx)
    other = lax.ppermute(mine, "c", swap)
    mine, other = (a.reshape(nzx, STEPS, held, NB) for a in (mine, other))
    both = jnp.stack([jnp.where(core == 0, mine, other), jnp.where(core == 0, other, mine)], axis=1)
    full = both.transpose(2, 0, 1, 3, 4).reshape(STEPS, local, NB)

    picked, tops, select = pl.pallas_call(
        prep_kernel,
        out_shape=(
            jax.ShapeDtypeStruct((TOP, width), BF),
            jax.ShapeDtypeStruct((TOP, width), BF),
            jax.ShapeDtypeStruct((2 * NB, start_of(STEPS)), BF),
        ),
        in_specs=[SM, VM, VM, VM],
        out_specs=(VM, VM, VM),
        cost_estimate=cost(2 * TOP * local * width, 8 << 20),
    )(first1, pivots, pivots.reshape(TOP, 1), matrix)
    share = jnp.concatenate([picked.reshape(ny, TOP // ny, width), tops.reshape(ny, TOP // ny, width)], axis=1)
    got = lax.all_to_all(share, "y", 0, 0, tiled=True)
    content = spread(got.astype(F32).sum(0).astype(BF), "y", ny)

    idx = []
    for k, j in PAIRS:
        for rows in (pivots[k], k * NB + jnp.arange(NB, dtype=jnp.int32)):
            here = rows - first
            idx.append(jnp.where((here >= 0) & (here < local), here + j * local, -1))
    per_dev = len(idx) * NB // (nzx * nc)
    chunk = -(-per_dev // CHUNK) * CHUNK
    idx = jnp.concatenate(idx + [jnp.full((chunk * nzx * nc - len(idx) * NB,), -1, jnp.int32)])
    idx = lax.dynamic_slice(idx, ((core * nzx + zx) * chunk,), (chunk,))
    part = jnp.take(full.reshape(STEPS * local, NB), jnp.maximum(idx, 0), axis=0)
    part = jnp.where((idx >= 0)[:, None], part, jnp.zeros((), BF))
    part = spread(part, "y", ny).astype(F32).reshape(ny, chunk, NB).sum(0).astype(BF)
    low_mine = spread(part, ("z", "x"), nzx)
    low_other = lax.ppermute(low_mine, "c", swap)

    factor, kept = pl.pallas_call(
        rows_kernel,
        out_shape=(jax.ShapeDtypeStruct((local, 2 * TOP), BF), jax.ShapeDtypeStruct((local, width), BF)),
        in_specs=[SM, VM, VM, VM],
        out_specs=(VM, VM),
        cost_estimate=cost(2 * TOP * local * NB, 12 << 20),
    )(first1, pivots, full, matrix)

    return pl.pallas_call(
        solve_kernel,
        out_shape=jax.ShapeDtypeStruct((local, width), BF),
        in_specs=[SM, VM, VM, VM, VM, VM, ANY, ANY],
        out_specs=VM,
        scratch_shapes=[
            pltpu.VMEM((2, nzx * chunk, NB), BF),
            pltpu.VMEM((2 * NB, 2 * NB * (STEPS - 1)), BF),
            pltpu.VMEM((2 * TOP, width), BF),
            pltpu.VMEM((local, 2 * TOP), BF),
            pltpu.VMEM((local, width), BF),
            pltpu.SemaphoreType.DMA((2,)),
        ],
        cost_estimate=cost(4 * TOP * local * width, 16 << 20),
    )(core1, content.reshape(ny, 2 * TOP // ny, width), low_mine.reshape(nzx, chunk, NB), low_other.reshape(nzx, chunk, NB),
      inverses, select, factor, kept)


def solution(mesh):
    ny, npb = mesh.devices.shape
    nz, nx, nc = (8, 4, 2) if npb == 64 else (1, npb // 2, 2)
    fine = Mesh(mesh.devices.reshape(ny, nz, nx, nc), ("y", "z", "x", "c"))
    cols = ("z", "x", "c")
    in_specs = (P("y", cols), P(None, ("y",) + cols, None), P(), P())
    return jax.shard_map(
        functools.partial(per_device, ny, nz * nx, nc), mesh=fine, in_specs=in_specs, out_specs=P("y", cols), check_vma=False
    )
```

```python
import functools

import jax
import jax.numpy as jnp
from jax import lax
from jax.experimental import pallas as pl
from jax.experimental.pallas import tpu as pltpu
from jax.sharding import Mesh
from jax.sharding import PartitionSpec as P

NB = 128
STEPS = 6
TOP = NB * STEPS
PAIRS = [(k, j) for k in range(1, STEPS) for j in range(k)]
CHUNK = 64
BF = jnp.bfloat16
F32 = jnp.float32
VM = pl.BlockSpec(memory_space=pltpu.VMEM)
SM = pl.BlockSpec(memory_space=pltpu.SMEM)
ANY = pl.BlockSpec(memory_space=pl.ANY)


def start_of(k):
    return 2 * NB * (k * (k - 1) // 2)


def iota(shape, dim):
    return lax.broadcasted_iota(jnp.int32, shape, dim)


def prep_kernel(first_ref, me_ref, rows_ref, cols_ref, matrix_ref, select_ref, *rest):
    piece_refs, fresh_ref = rest[:-1], rest[-1]
    parts = len(piece_refs)
    first, me = first_ref[0], me_ref[0]
    ones = jnp.ones((NB, NB), BF)
    local, width = matrix_ref.shape
    each = TOP // parts
    for k in range(STEPS):
        ids = jnp.concatenate([iota((NB, NB), 0) + k * NB, jnp.broadcast_to(cols_ref[k * NB:(k + 1) * NB, :], (NB, NB))])
        found = jnp.zeros((2 * NB, NB), F32)
        for j in reversed(range(k)):
            at = start_of(k) + 2 * NB * j
            same = jnp.where(ids == rows_ref[j:j + 1, :], 1.0, 0.0).astype(F32)
            live = 1.0 - found
            select_ref[:, at:at + NB] = (same * live).astype(BF)
            select_ref[:, at + NB:at + 2 * NB] = (-live).astype(BF)
            hit = jnp.dot(same.astype(BF), ones, preferred_element_type=F32)
            found = jnp.maximum(found, hit)
        fresh_ref[0, k * NB:(k + 1) * NB, :] = found[:NB]
        fresh_ref[1, k * NB:(k + 1) * NB, :] = found[NB:]
    for s in range(parts):
        at = pl.multiple_of(lax.rem(me + s, parts) * each, each)
        where = cols_ref[pl.ds(at, each), :] - first
        hot = jnp.where(iota((each, local), 1) == where, 1.0, 0.0).astype(BF)
        row = jnp.dot(hot, matrix_ref[...], preferred_element_type=F32)
        fresh = fresh_ref[1, pl.ds(at, each), :] < 0.5
        mine = (fresh_ref[0, pl.ds(at, each), :] < 0.5) & (first == 0)
        for c in range(0, width, NB):
            piece_refs[s][:each, c:c + NB] = jnp.where(fresh, row[:, c:c + NB], 0.0).astype(BF)
            top = matrix_ref[pl.ds(at, each), c:c + NB].astype(F32)
            piece_refs[s][each:, c:c + NB] = jnp.where(mine, top, 0.0).astype(BF)


def rows_kernel(first_ref, rows_ref, panels_ref, matrix_ref, factor_ref, kept_ref):
    ones = jnp.ones((NB, NB), BF)
    height = 2 * NB

    def one(step, carry):
        at = pl.multiple_of(step * height, height)
        ids = iota((height, NB), 0) + first_ref[0] + at
        is_top = ids < TOP
        found = jnp.zeros((height, NB), F32)
        for j in reversed(range(STEPS)):
            same = jnp.where((ids == rows_ref[j:j + 1, :]) & ~is_top, 1.0, 0.0).astype(F32)
            live = 1.0 - found
            factor_ref[pl.ds(at, height), 2 * NB * j:2 * NB * j + NB] = (same * live).astype(BF)
            diag = jnp.where(ids - NB * j == iota((height, NB), 1), 1.0, 0.0).astype(F32)
            lower = -live * panels_ref[j, pl.ds(at, height), :].astype(F32)
            factor_ref[pl.ds(at, height), 2 * NB * j + NB:2 * NB * (j + 1)] = jnp.where(is_top, diag, lower).astype(BF)
            hit = jnp.dot(same.astype(BF), ones, preferred_element_type=F32)
            found = jnp.maximum(found, hit)
        fresh = (found < 0.5) & ~is_top
        for c in range(0, matrix_ref.shape[1], NB):
            old = matrix_ref[pl.ds(at, height), c:c + NB].astype(F32)
            kept_ref[pl.ds(at, height), c:c + NB] = jnp.where(fresh, old, 0.0).astype(BF)
        return carry

    lax.fori_loop(0, matrix_ref.shape[0] // height, one, 0)


def solve_kernel(core_ref, me_ref, mine_ref, other_ref, inverses_ref, select_ref, factor_hbm, kept_hbm, *rest):
    content_refs, (out_ref, low, coef, state, factor, kept, content, sems) = rest[:-8], rest[-8:]
    loads = [pltpu.make_async_copy(factor_hbm, factor, sems.at[0]), pltpu.make_async_copy(kept_hbm, kept, sems.at[1])]
    for load in loads:
        load.start()
    half = low.shape[1]
    core = core_ref[0]
    low[core] = mine_ref[...].reshape(half, NB)
    low[1 - core] = other_ref[...].reshape(half, NB)
    parts = len(content_refs)
    each = TOP // parts
    for i, ref in enumerate(content_refs):
        at = pl.multiple_of(lax.rem(me_ref[0] + parts - i, parts) * each, each)
        content[1, pl.ds(at, each), :] = ref[:each]
        content[0, pl.ds(at, each), :] = ref[each:]
    for k in range(STEPS):
        x = content[:, k * NB:(k + 1) * NB, :].reshape(2 * NB, -1).astype(F32)
        if k:
            for j in range(k):
                at = start_of(k) + 2 * NB * j
                t = 2 * PAIRS.index((k, j))
                b0, b1 = t * NB, (t + 1) * NB
                block = jnp.concatenate([low[b1 // half, b1 % half:b1 % half + NB, :], low[b0 // half, b0 % half:b0 % half + NB, :]])
                coef[:, 2 * NB * j:2 * NB * j + NB] = select_ref[:, at:at + NB]
                coef[:, 2 * NB * j + NB:2 * NB * (j + 1)] = select_ref[:, at + NB:at + 2 * NB] * block
            x = x + jnp.dot(coef[:, :2 * NB * k], state[:2 * NB * k, :], preferred_element_type=F32)
        y = x.astype(BF)
        state[2 * NB * k:2 * NB * k + NB, :] = y[:NB]
        inv = inverses_ref[k]
        hi = inv.astype(BF)
        rest = inv - hi.astype(F32)
        mid = rest.astype(BF)
        lo = (rest - mid.astype(F32)).astype(BF)
        v = y[NB:]
        upper = jnp.dot(hi, v, preferred_element_type=F32) + (
            jnp.dot(mid, v, preferred_element_type=F32) + jnp.dot(lo, v, preferred_element_type=F32))
        state[2 * NB * k + NB:2 * NB * (k + 1), :] = upper.astype(BF)
    for load in loads:
        load.wait()

    def one(step, carry):
        at = pl.multiple_of(step * 2 * NB, 2 * NB)
        new = jnp.dot(factor[pl.ds(at, 2 * NB), :], state[...], preferred_element_type=F32)
        out_ref[pl.ds(at, 2 * NB), :] = (kept[pl.ds(at, 2 * NB), :].astype(F32) + new).astype(BF)
        return carry

    lax.fori_loop(0, out_ref.shape[0] // (2 * NB), one, 0)


def cost(flops, nbytes):
    return pl.CostEstimate(flops=flops, bytes_accessed=nbytes, transcendentals=0)


def spread(x, axes, parts):
    return lax.all_to_all(jnp.broadcast_to(x[None], (parts,) + x.shape), axes, 0, 0, tiled=True)


def shift(x, n, s):
    return lax.ppermute(x, "y", [(i, (i + s) % n) for i in range(n)])


def per_device(ny, nz, nx, nc, matrix, panels, inverses, pivots):
    nzx = nz * nx
    local, width = matrix.shape
    held = panels.shape[1]
    y, core = lax.axis_index("y"), lax.axis_index("c")
    zx = lax.axis_index(("z", "x"))
    first = y * local
    swap = [(0, 1), (1, 0)]
    first1 = first.reshape(1).astype(jnp.int32)
    me1, core1 = (a.reshape(1).astype(jnp.int32) for a in (y, core))

    each = TOP // ny
    select, *pieces = pl.pallas_call(
        prep_kernel,
        out_shape=(jax.ShapeDtypeStruct((2 * NB, start_of(STEPS)), BF),) + (jax.ShapeDtypeStruct((2 * each, width), BF),) * ny,
        in_specs=[SM, SM, VM, VM, VM],
        out_specs=(VM,) * (ny + 1),
        scratch_shapes=[pltpu.VMEM((2, TOP, NB), F32)],
        cost_estimate=cost(2 * TOP * local * width, 8 << 20),
    )(first1, me1, pivots, pivots.reshape(TOP, 1), matrix)

    mine = spread(panels.reshape(STEPS * held, NB), "z", nz)
    mine, *pieces = lax.optimization_barrier((mine, *pieces))
    mine = spread(mine, "x", nx)
    content = sum(pieces[:1] + [shift(pieces[s], ny, s) for s in range(1, ny)])
    mine, content = lax.optimization_barrier((mine, content))
    contents = [content] + [shift(content, ny, s) for s in range(1, ny)]
    other = lax.ppermute(mine, "c", swap)
    mine, other = (a.reshape(nx, nz, STEPS, held, NB) for a in (mine, other))
    both = jnp.stack([jnp.where(core == 0, mine, other), jnp.where(core == 0, other, mine)])
    full = both.transpose(3, 2, 1, 0, 4, 5).reshape(STEPS, local, NB)

    idx = []
    for k, j in PAIRS:
        for rows in (pivots[k], k * NB + jnp.arange(NB, dtype=jnp.int32)):
            here = rows - first
            idx.append(jnp.where((here >= 0) & (here < local), here + j * local, -1))
    per_dev = len(idx) * NB // (nzx * nc)
    chunk = -(-per_dev // CHUNK) * CHUNK
    idx = jnp.concatenate(idx + [jnp.full((chunk * nzx * nc - len(idx) * NB,), -1, jnp.int32)])
    idx = lax.dynamic_slice(idx, ((core * nzx + zx) * chunk,), (chunk,))
    part = jnp.take(full.reshape(STEPS * local, NB), jnp.maximum(idx, 0), axis=0)
    part = jnp.where((idx >= 0)[:, None], part, jnp.zeros((), BF))
    part = spread(part, "y", ny).reshape(ny, chunk, NB).astype(F32).sum(0).astype(BF)
    part, *contents[1:4] = lax.optimization_barrier((part, *contents[1:4]))
    low_mine = spread(part, ("z", "x"), nzx)
    low_mine, *contents[4:] = lax.optimization_barrier((low_mine, *contents[4:]))
    low_other = lax.ppermute(low_mine, "c", swap)

    factor, kept = pl.pallas_call(
        rows_kernel,
        out_shape=(jax.ShapeDtypeStruct((local, 2 * TOP), BF), jax.ShapeDtypeStruct((local, width), BF)),
        in_specs=[SM, VM, VM, VM],
        out_specs=(VM, VM),
        cost_estimate=cost(2 * TOP * local * NB, 12 << 20),
    )(first1, pivots, full, matrix)

    return pl.pallas_call(
        solve_kernel,
        out_shape=jax.ShapeDtypeStruct((local, width), BF),
        in_specs=[SM, SM, VM, VM, VM, VM, ANY, ANY] + [VM] * ny,
        out_specs=VM,
        scratch_shapes=[
            pltpu.VMEM((2, nzx * chunk, NB), BF),
            pltpu.VMEM((2 * NB, 2 * NB * (STEPS - 1)), BF),
            pltpu.VMEM((2 * TOP, width), BF),
            pltpu.VMEM((local, 2 * TOP), BF),
            pltpu.VMEM((local, width), BF),
            pltpu.VMEM((2, TOP, width), BF),
            pltpu.SemaphoreType.DMA((2,)),
        ],
        cost_estimate=cost(4 * TOP * local * width, 16 << 20),
    )(core1, me1, low_mine.reshape(nzx, chunk, NB), low_other.reshape(nzx, chunk, NB),
      inverses, select, factor, kept, *contents)


def solution(mesh):
    ny, npb = mesh.devices.shape
    nz, nx, nc = (8, 4, 2) if npb == 64 else (1, npb // 2, 2)
    fine = Mesh(mesh.devices.reshape(ny, nz, nx, nc), ("y", "z", "x", "c"))
    cols = ("z", "x", "c")
    in_specs = (P("y", cols), P(None, ("y",) + cols, None), P(), P())
    return jax.shard_map(
        functools.partial(per_device, ny, nz, nx, nc), mesh=fine, in_specs=in_specs, out_specs=P("y", cols), check_vma=False
    )
```

```python
import functools

import jax
import jax.numpy as jnp
from jax import lax
from jax.experimental import pallas as pl
from jax.experimental.pallas import tpu as pltpu
from jax.sharding import Mesh
from jax.sharding import PartitionSpec as P

NB = 128
STEPS = 6
TOP = NB * STEPS
PAIRS = [(k, j) for k in range(1, STEPS) for j in range(k)]
CHUNK = 64
BF = jnp.bfloat16
F32 = jnp.float32
VM = pl.BlockSpec(memory_space=pltpu.VMEM)
SM = pl.BlockSpec(memory_space=pltpu.SMEM)
ANY = pl.BlockSpec(memory_space=pl.ANY)


def start_of(k):
    return 2 * NB * (k * (k - 1) // 2)


def iota(shape, dim):
    return lax.broadcasted_iota(jnp.int32, shape, dim)


def prep_kernel(first_ref, rows_ref, cols_ref, matrix_ref, share_ref, select_ref):
    first = first_ref[0]
    ones = jnp.ones((NB, NB), BF)
    local, width = matrix_ref.shape
    for k in range(STEPS):
        ids = jnp.concatenate([iota((NB, NB), 0) + k * NB, jnp.broadcast_to(cols_ref[k * NB:(k + 1) * NB, :], (NB, NB))])
        found = jnp.zeros((2 * NB, NB), F32)
        for j in reversed(range(k)):
            at = start_of(k) + 2 * NB * j
            same = jnp.where(ids == rows_ref[j:j + 1, :], 1.0, 0.0).astype(F32)
            live = 1.0 - found
            select_ref[:, at:at + NB] = (same * live).astype(BF)
            select_ref[:, at + NB:at + 2 * NB] = (-live).astype(BF)
            hit = jnp.dot(same.astype(BF), ones, preferred_element_type=F32)
            found = jnp.maximum(found, hit)
        fresh = found < 0.5
        at = k * NB
        hot = jnp.where(iota((NB, local), 1) == cols_ref[at:at + NB, :] - first, 1.0, 0.0).astype(BF)
        row = jnp.dot(hot, matrix_ref[...], preferred_element_type=F32)
        mine = fresh[:NB] & (first == 0)
        for c in range(0, width, NB):
            top = matrix_ref[at:at + NB, c:c + NB].astype(F32)
            share_ref[0, at:at + NB, c:c + NB] = jnp.where(mine, top, 0.0).astype(BF)
            share_ref[1, at:at + NB, c:c + NB] = jnp.where(fresh[NB:], row[:, c:c + NB], 0.0).astype(BF)


def rows_kernel(first_ref, rows_ref, panels_ref, matrix_ref, factor_ref, kept_ref):
    ones = jnp.ones((NB, NB), BF)
    height = 2 * NB

    def one(step, carry):
        at = pl.multiple_of(step * height, height)
        ids = iota((height, NB), 0) + first_ref[0] + at
        is_top = ids < TOP
        found = jnp.zeros((height, NB), F32)
        for j in reversed(range(STEPS)):
            same = jnp.where((ids == rows_ref[j:j + 1, :]) & ~is_top, 1.0, 0.0).astype(F32)
            live = 1.0 - found
            factor_ref[pl.ds(at, height), 2 * NB * j:2 * NB * j + NB] = (same * live).astype(BF)
            diag = jnp.where(ids - NB * j == iota((height, NB), 1), 1.0, 0.0).astype(F32)
            lower = -live * panels_ref[j, pl.ds(at, height), :].astype(F32)
            factor_ref[pl.ds(at, height), 2 * NB * j + NB:2 * NB * (j + 1)] = jnp.where(is_top, diag, lower).astype(BF)
            hit = jnp.dot(same.astype(BF), ones, preferred_element_type=F32)
            found = jnp.maximum(found, hit)
        fresh = (found < 0.5) & ~is_top
        for c in range(0, matrix_ref.shape[1], NB):
            old = matrix_ref[pl.ds(at, height), c:c + NB].astype(F32)
            kept_ref[pl.ds(at, height), c:c + NB] = jnp.where(fresh, old, 0.0).astype(BF)
        return carry

    lax.fori_loop(0, matrix_ref.shape[0] // height, one, 0)


def solve_kernel(core_ref, content, mine_ref, other_ref, inverses_ref, select_ref, factor_hbm, kept_hbm, out_ref,
                 low, coef, state, factor, kept, sems):
    loads = [pltpu.make_async_copy(factor_hbm, factor, sems.at[0]), pltpu.make_async_copy(kept_hbm, kept, sems.at[1])]
    for load in loads:
        load.start()
    half = low.shape[1]
    core = core_ref[0]
    low[core] = mine_ref[...].reshape(half, NB)
    low[1 - core] = other_ref[...].reshape(half, NB)
    for k in range(STEPS):
        x = content[:, k * NB:(k + 1) * NB, :].reshape(2 * NB, -1).astype(F32)
        if k:
            for j in range(k):
                at = start_of(k) + 2 * NB * j
                t = 2 * PAIRS.index((k, j))
                b0, b1 = t * NB, (t + 1) * NB
                block = jnp.concatenate([low[b1 // half, b1 % half:b1 % half + NB, :], low[b0 // half, b0 % half:b0 % half + NB, :]])
                coef[:, 2 * NB * j:2 * NB * j + NB] = select_ref[:, at:at + NB]
                coef[:, 2 * NB * j + NB:2 * NB * (j + 1)] = select_ref[:, at + NB:at + 2 * NB] * block
            x = x + jnp.dot(coef[:, :2 * NB * k], state[:2 * NB * k, :], preferred_element_type=F32)
        y = x.astype(BF)
        state[2 * NB * k:2 * NB * k + NB, :] = y[:NB]
        inv = inverses_ref[k]
        hi = inv.astype(BF)
        rest = inv - hi.astype(F32)
        mid = rest.astype(BF)
        lo = (rest - mid.astype(F32)).astype(BF)
        v = y[NB:]
        upper = jnp.dot(hi, v, preferred_element_type=F32) + (
            jnp.dot(mid, v, preferred_element_type=F32) + jnp.dot(lo, v, preferred_element_type=F32))
        state[2 * NB * k + NB:2 * NB * (k + 1), :] = upper.astype(BF)
    for load in loads:
        load.wait()

    def one(step, carry):
        at = pl.multiple_of(step * 2 * NB, 2 * NB)
        new = jnp.dot(factor[pl.ds(at, 2 * NB), :], state[...], preferred_element_type=F32)
        out_ref[pl.ds(at, 2 * NB), :] = (kept[pl.ds(at, 2 * NB), :].astype(F32) + new).astype(BF)
        return carry

    lax.fori_loop(0, out_ref.shape[0] // (2 * NB), one, 0)


def cost(flops, nbytes):
    return pl.CostEstimate(flops=flops, bytes_accessed=nbytes, transcendentals=0)


def spread(x, axes, parts):
    return lax.all_to_all(jnp.broadcast_to(x[None], (parts,) + x.shape), axes, 0, 0, tiled=True)


def per_device(ny, nz, nx, nc, matrix, panels, inverses, pivots):
    nzx = nz * nx
    local, width = matrix.shape
    held = panels.shape[1]
    y, core = lax.axis_index("y"), lax.axis_index("c")
    zx = lax.axis_index(("z", "x"))
    first = y * local
    swap = [(0, 1), (1, 0)]
    first1 = first.reshape(1).astype(jnp.int32)
    core1 = core.reshape(1).astype(jnp.int32)

    share, select = pl.pallas_call(
        prep_kernel,
        out_shape=(jax.ShapeDtypeStruct((2, TOP, width), BF), jax.ShapeDtypeStruct((2 * NB, start_of(STEPS)), BF)),
        in_specs=[SM, VM, VM, VM],
        out_specs=(VM, VM),
        cost_estimate=cost(2 * TOP * local * width, 8 << 20),
    )(first1, pivots, pivots.reshape(TOP, 1), matrix)
    content = lax.psum(share, "y")

    mine = spread(panels.reshape(STEPS * held, NB), "z", nz)
    mine, pivots, _ = lax.optimization_barrier((mine, pivots, share))

    def gather(mine, pivots):
        mine = spread(mine, "x", nx)
        other = lax.ppermute(mine, "c", swap)
        mine, other = (a.reshape(nx, nz, STEPS, held, NB) for a in (mine, other))
        both = jnp.stack([jnp.where(core == 0, mine, other), jnp.where(core == 0, other, mine)])
        full = both.transpose(3, 2, 1, 0, 4, 5).reshape(STEPS, local, NB)

        idx = []
        for k, j in PAIRS:
            for rows in (pivots[k], k * NB + jnp.arange(NB, dtype=jnp.int32)):
                here = rows - first
                idx.append(jnp.where((here >= 0) & (here < local), here + j * local, -1))
        per_dev = len(idx) * NB // (nzx * nc)
        chunk = -(-per_dev // CHUNK) * CHUNK
        idx = jnp.concatenate(idx + [jnp.full((chunk * nzx * nc - len(idx) * NB,), -1, jnp.int32)])
        idx = lax.dynamic_slice(idx, ((core * nzx + zx) * chunk,), (chunk,))
        part = jnp.take(full.reshape(STEPS * local, NB), jnp.maximum(idx, 0), axis=0)
        part = jnp.where((idx >= 0)[:, None], part, jnp.zeros((), BF))
        part = spread(part, "y", ny).reshape(ny, chunk, NB).astype(F32).sum(0).astype(BF)
        low_mine = spread(part, ("z", "x"), nzx)
        low_other = lax.ppermute(low_mine, "c", swap)

        factor, kept = pl.pallas_call(
            rows_kernel,
            out_shape=(jax.ShapeDtypeStruct((local, 2 * TOP), BF), jax.ShapeDtypeStruct((local, width), BF)),
            in_specs=[SM, VM, VM, VM],
            out_specs=(VM, VM),
            cost_estimate=cost(2 * TOP * local * NB, 12 << 20),
        )(first1, pivots, full, matrix)
        return low_mine, low_other, factor, kept

    def nothing(mine, pivots):
        return tuple(jnp.zeros(o.shape, o.dtype) for o in jax.eval_shape(gather, mine, pivots))

    low_mine, low_other, factor, kept = lax.cond(pivots[0, 0] > 0, gather, nothing, mine, pivots)

    chunk = low_mine.size // (nzx * NB)
    return pl.pallas_call(
        solve_kernel,
        out_shape=jax.ShapeDtypeStruct((local, width), BF),
        in_specs=[SM, VM, VM, VM, VM, VM, ANY, ANY],
        out_specs=VM,
        scratch_shapes=[
            pltpu.VMEM((2, nzx * chunk, NB), BF),
            pltpu.VMEM((2 * NB, 2 * NB * (STEPS - 1)), BF),
            pltpu.VMEM((2 * TOP, width), BF),
            pltpu.VMEM((local, 2 * TOP), BF),
            pltpu.VMEM((local, width), BF),
            pltpu.SemaphoreType.DMA((2,)),
        ],
        cost_estimate=cost(4 * TOP * local * width, 16 << 20),
    )(core1, content, low_mine.reshape(nzx, chunk, NB), low_other.reshape(nzx, chunk, NB),
      inverses, select, factor, kept)


def solution(mesh):
    ny, npb = mesh.devices.shape
    nz, nx, nc = (8, 4, 2) if npb == 64 else (1, npb // 2, 2)
    fine = Mesh(mesh.devices.reshape(ny, nz, nx, nc), ("y", "z", "x", "c"))
    cols = ("z", "x", "c")
    in_specs = (P("y", cols), P(None, ("y",) + cols, None), P(), P())
    return jax.shard_map(
        functools.partial(per_device, ny, nz, nx, nc), mesh=fine, in_specs=in_specs, out_specs=P("y", cols), check_vma=False
    )
```

```python
import functools

import jax
import jax.numpy as jnp
from jax import lax
from jax.experimental import pallas as pl
from jax.experimental.pallas import tpu as pltpu
from jax.sharding import Mesh
from jax.sharding import PartitionSpec as P

NB = 128
STEPS = 6
TOP = NB * STEPS
PAIRS = [(k, j) for k in range(1, STEPS) for j in range(k)]
CHUNK = 64
BF = jnp.bfloat16
F32 = jnp.float32
VM = pl.BlockSpec(memory_space=pltpu.VMEM)
SM = pl.BlockSpec(memory_space=pltpu.SMEM)
ANY = pl.BlockSpec(memory_space=pl.ANY)


def start_of(k):
    return 2 * NB * (k * (k - 1) // 2)


def iota(shape, dim):
    return lax.broadcasted_iota(jnp.int32, shape, dim)


def columns(row):
    return jnp.broadcast_to(row.astype(F32), (NB, NB)).T.astype(jnp.int32)


def masks(k, rows_ref):
    ones = jnp.ones((NB, NB), BF)
    ids = jnp.concatenate([iota((NB, NB), 0) + k * NB, columns(rows_ref[k:k + 1, :])])
    found = jnp.zeros((2 * NB, NB), F32)
    out = []
    for j in reversed(range(k)):
        same = jnp.where(ids == rows_ref[j:j + 1, :], 1.0, 0.0).astype(F32)
        live = 1.0 - found
        out.append((j, same * live, live))
        hit = jnp.dot(same.astype(BF), ones, preferred_element_type=F32)
        found = jnp.maximum(found, hit)
    return ids, out, found < 0.5


def share_kernel(first_ref, rows_ref, matrix_ref, share_ref, hot):
    first = first_ref[0]
    local, width = matrix_ref.shape
    for k in range(STEPS):
        ids, _, fresh = masks(k, rows_ref)
        at = k * NB
        where = ids[NB:] - first
        for c in range(0, local, NB):
            hot[:, c:c + NB] = jnp.where(iota((NB, NB), 1) + c == where, 1.0, 0.0).astype(BF)
        row = jnp.dot(hot[...], matrix_ref[...], preferred_element_type=F32)
        mine = fresh[:NB] & (first == 0)
        for c in range(0, width, NB):
            top = matrix_ref[at:at + NB, c:c + NB].astype(F32)
            share_ref[0, at:at + NB, c:c + NB] = jnp.where(mine, top, 0.0).astype(BF)
            share_ref[1, at:at + NB, c:c + NB] = jnp.where(fresh[NB:], row[:, c:c + NB], 0.0).astype(BF)


def rows_kernel(first_ref, rows_ref, panels_ref, matrix_ref, factor_ref, kept_ref, select_ref):
    for k in range(1, STEPS):
        for j, same, live in masks(k, rows_ref)[1]:
            at = start_of(k) + 2 * NB * j
            select_ref[:, at:at + NB] = same.astype(BF)
            select_ref[:, at + NB:at + 2 * NB] = (-live).astype(BF)
    ones = jnp.ones((NB, NB), BF)
    height = 2 * NB

    def one(step, carry):
        at = pl.multiple_of(step * height, height)
        ids = iota((height, NB), 0) + first_ref[0] + at
        is_top = ids < TOP
        found = jnp.zeros((height, NB), F32)
        for j in reversed(range(STEPS)):
            same = jnp.where((ids == rows_ref[j:j + 1, :]) & ~is_top, 1.0, 0.0).astype(F32)
            live = 1.0 - found
            factor_ref[pl.ds(at, height), 2 * NB * j:2 * NB * j + NB] = (same * live).astype(BF)
            diag = jnp.where(ids - NB * j == iota((height, NB), 1), 1.0, 0.0).astype(F32)
            lower = -live * panels_ref[j, pl.ds(at, height), :].astype(F32)
            factor_ref[pl.ds(at, height), 2 * NB * j + NB:2 * NB * (j + 1)] = jnp.where(is_top, diag, lower).astype(BF)
            hit = jnp.dot(same.astype(BF), ones, preferred_element_type=F32)
            found = jnp.maximum(found, hit)
        fresh = (found < 0.5) & ~is_top
        for c in range(0, matrix_ref.shape[1], NB):
            old = matrix_ref[pl.ds(at, height), c:c + NB].astype(F32)
            kept_ref[pl.ds(at, height), c:c + NB] = jnp.where(fresh, old, 0.0).astype(BF)
        return carry

    lax.fori_loop(0, matrix_ref.shape[0] // height, one, 0)


def solve_kernel(core_ref, content, mine_ref, other_ref, inverses_ref, select_ref, factor_hbm, kept_hbm, out_ref,
                 low, coef, state, factor, kept, sems):
    loads = [pltpu.make_async_copy(factor_hbm, factor, sems.at[0]), pltpu.make_async_copy(kept_hbm, kept, sems.at[1])]
    for load in loads:
        load.start()
    half = low.shape[1]
    core = core_ref[0]
    low[core] = mine_ref[...].reshape(half, NB)
    low[1 - core] = other_ref[...].reshape(half, NB)
    for k in range(STEPS):
        x = content[:, k * NB:(k + 1) * NB, :].reshape(2 * NB, -1).astype(F32)
        if k:
            for j in range(k):
                at = start_of(k) + 2 * NB * j
                t = 2 * PAIRS.index((k, j))
                b0, b1 = t * NB, (t + 1) * NB
                block = jnp.concatenate([low[b1 // half, b1 % half:b1 % half + NB, :], low[b0 // half, b0 % half:b0 % half + NB, :]])
                coef[:, 2 * NB * j:2 * NB * j + NB] = select_ref[:, at:at + NB]
                coef[:, 2 * NB * j + NB:2 * NB * (j + 1)] = select_ref[:, at + NB:at + 2 * NB] * block
            x = x + jnp.dot(coef[:, :2 * NB * k], state[:2 * NB * k, :], preferred_element_type=F32)
        y = x.astype(BF)
        state[2 * NB * k:2 * NB * k + NB, :] = y[:NB]
        inv = inverses_ref[k]
        hi = inv.astype(BF)
        rest = inv - hi.astype(F32)
        mid = rest.astype(BF)
        lo = (rest - mid.astype(F32)).astype(BF)
        v = y[NB:]
        upper = jnp.dot(hi, v, preferred_element_type=F32) + (
            jnp.dot(mid, v, preferred_element_type=F32) + jnp.dot(lo, v, preferred_element_type=F32))
        state[2 * NB * k + NB:2 * NB * (k + 1), :] = upper.astype(BF)
    for load in loads:
        load.wait()

    def one(step, carry):
        at = pl.multiple_of(step * 2 * NB, 2 * NB)
        new = jnp.dot(factor[pl.ds(at, 2 * NB), :], state[...], preferred_element_type=F32)
        out_ref[pl.ds(at, 2 * NB), :] = (kept[pl.ds(at, 2 * NB), :].astype(F32) + new).astype(BF)
        return carry

    lax.fori_loop(0, out_ref.shape[0] // (2 * NB), one, 0)


def cost(flops, nbytes):
    return pl.CostEstimate(flops=flops, bytes_accessed=nbytes, transcendentals=0)


def spread(x, axes, parts):
    return lax.all_to_all(jnp.broadcast_to(x[None], (parts,) + x.shape), axes, 0, 0, tiled=True)


def per_device(ny, nz, nx, nc, matrix, panels, inverses, pivots):
    nzx = nz * nx
    local, width = matrix.shape
    held = panels.shape[1]
    y, core = lax.axis_index("y"), lax.axis_index("c")
    zx = lax.axis_index(("z", "x"))
    first = y * local
    swap = [(0, 1), (1, 0)]
    first1 = first.reshape(1).astype(jnp.int32)
    core1 = core.reshape(1).astype(jnp.int32)

    share = pl.pallas_call(
        share_kernel,
        out_shape=jax.ShapeDtypeStruct((2, TOP, width), BF),
        in_specs=[SM, VM, VM],
        out_specs=VM,
        scratch_shapes=[pltpu.VMEM((NB, local), BF)],
        cost_estimate=cost(2 * TOP * local * width, 4 << 20),
    )(first1, pivots, matrix)
    content = lax.psum(share, "y")
    panels, pivots, _ = lax.optimization_barrier((panels, pivots, share))

    def gather(panels, pivots):
        mine = spread(panels.reshape(STEPS * held, NB), "z", nz)
        mine = spread(mine, "x", nx)

        idx = []
        for k, j in PAIRS:
            for rows in (pivots[k], k * NB + jnp.arange(NB, dtype=jnp.int32)):
                here = rows - first
                pb = here // held
                at = ((pb // nc % nx * nz + pb // nc // nx) * STEPS + j) * held + here % held
                idx.append(jnp.where((here >= 0) & (here < local) & (pb % nc == core), at, -1))
        chunk = -(-len(idx) * NB // (nzx * nc) // CHUNK) * CHUNK
        idx = jnp.concatenate(idx + [jnp.full((chunk * nzx * nc - len(idx) * NB,), -1, jnp.int32)])
        idx = lax.dynamic_slice(idx.reshape(nc, nzx, chunk), (0, zx, 0), (nc, 1, chunk)).reshape(nc * chunk)
        part = jnp.take(mine.reshape(-1, NB), jnp.maximum(idx, 0), axis=0)
        part = jnp.where((idx >= 0)[:, None], part, jnp.zeros((), BF)).reshape(1, nc, chunk, NB)
        part = jnp.broadcast_to(part, (ny, nc, chunk, NB)).reshape(ny * nc, chunk, NB)
        part = lax.all_to_all(part, ("y", "c"), 0, 0, tiled=True).astype(F32).sum(0).astype(BF)

        other = lax.ppermute(mine, "c", swap)
        part, other = lax.optimization_barrier((part, other))
        low_mine = spread(part, ("z", "x"), nzx)

        both = [a.reshape(nx, nz, STEPS, held, NB) for a in (mine, other)]
        both = jnp.stack([jnp.where(core == 0, both[0], both[1]), jnp.where(core == 0, both[1], both[0])])
        full = both.transpose(3, 2, 1, 0, 4, 5).reshape(STEPS, local, NB)
        factor, kept, select = pl.pallas_call(
            rows_kernel,
            out_shape=(
                jax.ShapeDtypeStruct((local, 2 * TOP), BF),
                jax.ShapeDtypeStruct((local, width), BF),
                jax.ShapeDtypeStruct((2 * NB, start_of(STEPS)), BF),
            ),
            in_specs=[SM, VM, VM, VM],
            out_specs=(VM, VM, VM),
            cost_estimate=cost(2 * TOP * local * NB, 12 << 20),
        )(first1, pivots, full, matrix)
        low_mine, factor, kept, select = lax.optimization_barrier((low_mine, factor, kept, select))
        return low_mine, lax.ppermute(low_mine, "c", swap), factor, kept, select

    def nothing(panels, pivots):
        return tuple(jnp.zeros(o.shape, o.dtype) for o in jax.eval_shape(gather, panels, pivots))

    low_mine, low_other, factor, kept, select = lax.cond(pivots[0, 0] > 0, gather, nothing, panels, pivots)

    chunk = low_mine.size // (nzx * NB)
    return pl.pallas_call(
        solve_kernel,
        out_shape=jax.ShapeDtypeStruct((local, width), BF),
        in_specs=[SM, VM, VM, VM, VM, VM, ANY, ANY],
        out_specs=VM,
        scratch_shapes=[
            pltpu.VMEM((2, nzx * chunk, NB), BF),
            pltpu.VMEM((2 * NB, 2 * NB * (STEPS - 1)), BF),
            pltpu.VMEM((2 * TOP, width), BF),
            pltpu.VMEM((local, 2 * TOP), BF),
            pltpu.VMEM((local, width), BF),
            pltpu.SemaphoreType.DMA((2,)),
        ],
        cost_estimate=cost(4 * TOP * local * width, 16 << 20),
    )(core1, content, low_mine.reshape(nzx, chunk, NB), low_other.reshape(nzx, chunk, NB),
      inverses, select, factor, kept)


def solution(mesh):
    ny, npb = mesh.devices.shape
    nz, nx, nc = (8, 4, 2) if npb == 64 else (1, npb // 2, 2)
    fine = Mesh(mesh.devices.reshape(ny, nz, nx, nc), ("y", "z", "x", "c"))
    cols = ("z", "x", "c")
    in_specs = (P("y", cols), P(None, ("y",) + cols, None), P(), P())
    return jax.shard_map(
        functools.partial(per_device, ny, nz, nx, nc), mesh=fine, in_specs=in_specs, out_specs=P("y", cols), check_vma=False
    )
```

```python
import functools

import jax
import jax.numpy as jnp
from jax import lax
from jax.experimental import pallas as pl
from jax.experimental.pallas import tpu as pltpu
from jax.sharding import Mesh
from jax.sharding import PartitionSpec as P

NB = 128
STEPS = 6
TOP = NB * STEPS
PAIRS = [(k, j) for k in range(1, STEPS) for j in range(k)]
CHUNK = 64
BLOCKS = 3
BF = jnp.bfloat16
F32 = jnp.float32
VM = pl.BlockSpec(memory_space=pltpu.VMEM)
SM = pl.BlockSpec(memory_space=pltpu.SMEM)
ANY = pl.BlockSpec(memory_space=pl.ANY)


def start_of(k):
    return 2 * NB * (k * (k - 1) // 2)


def iota(shape, dim):
    return lax.broadcasted_iota(jnp.int32, shape, dim)


def columns(row):
    return jnp.broadcast_to(row.astype(F32), (NB, NB)).T.astype(jnp.int32)


def masks(k, rows_ref):
    ones = jnp.ones((NB, NB), BF)
    ids = jnp.concatenate([iota((NB, NB), 0) + k * NB, columns(rows_ref[k:k + 1, :])])
    found = jnp.zeros((2 * NB, NB), F32)
    out = []
    for j in reversed(range(k)):
        same = jnp.where(ids == rows_ref[j:j + 1, :], 1.0, 0.0).astype(F32)
        live = 1.0 - found
        out.append((j, same * live, live))
        hit = jnp.dot(same.astype(BF), ones, preferred_element_type=F32)
        found = jnp.maximum(found, hit)
    return ids, out, found < 0.5


def share_kernel(first_ref, rows_ref, matrix_ref, share_ref, hot):
    first = first_ref[0]
    local, width = matrix_ref.shape
    fresh = []
    for k in range(STEPS):
        ids, _, new = masks(k, rows_ref)
        fresh.append(new)
        at = k * NB
        where = ids[NB:] - first
        for c in range(0, local, NB):
            hot[at:at + NB, c:c + NB] = jnp.where(iota((NB, NB), 1) + c == where, 1.0, 0.0).astype(BF)
    for c in range(0, width, NB):
        row = jnp.dot(hot[...], matrix_ref[:, c:c + NB], preferred_element_type=F32)
        for k in range(STEPS):
            at = k * NB
            top = matrix_ref[at:at + NB, c:c + NB].astype(F32)
            share_ref[0, at:at + NB, c:c + NB] = jnp.where(fresh[k][:NB] & (first == 0), top, 0.0).astype(BF)
            share_ref[1, at:at + NB, c:c + NB] = jnp.where(fresh[k][NB:], row[at:at + NB], 0.0).astype(BF)


def rows_kernel(first_ref, rows_ref, panels_ref, matrix_ref, inverses_ref, factor_ref, kept_ref, select_ref, parts_ref):
    for k in range(1, STEPS):
        for j, same, live in masks(k, rows_ref)[1]:
            at = start_of(k) + 2 * NB * j
            select_ref[:, at:at + NB] = same.astype(BF)
            select_ref[:, at + NB:at + 2 * NB] = (-live).astype(BF)
    for k in range(STEPS):
        rest = inverses_ref[k]
        for i in range(3):
            parts_ref[k, i * NB:(i + 1) * NB, :] = rest.astype(BF)
            rest = rest - rest.astype(BF).astype(F32)
    ones = jnp.ones((NB, NB), BF)
    height = 2 * NB

    def one(step, carry):
        at = pl.multiple_of(step * height, height)
        ids = iota((height, NB), 0) + first_ref[0] + at
        is_top = ids < TOP
        found = jnp.zeros((height, NB), F32)
        for j in reversed(range(STEPS)):
            same = jnp.where((ids == rows_ref[j:j + 1, :]) & ~is_top, 1.0, 0.0).astype(F32)
            live = 1.0 - found
            factor_ref[pl.ds(at, height), 2 * NB * j:2 * NB * j + NB] = (same * live).astype(BF)
            diag = jnp.where(ids - NB * j == iota((height, NB), 1), 1.0, 0.0).astype(F32)
            lower = -live * panels_ref[j, pl.ds(at, height), :].astype(F32)
            factor_ref[pl.ds(at, height), 2 * NB * j + NB:2 * NB * (j + 1)] = jnp.where(is_top, diag, lower).astype(BF)
            hit = jnp.dot(same.astype(BF), ones, preferred_element_type=F32)
            found = jnp.maximum(found, hit)
        fresh = (found < 0.5) & ~is_top
        for c in range(0, matrix_ref.shape[1], NB):
            old = matrix_ref[pl.ds(at, height), c:c + NB].astype(F32)
            kept_ref[pl.ds(at, height), c:c + NB] = jnp.where(fresh, old, 0.0).astype(BF)
        return carry

    lax.fori_loop(0, matrix_ref.shape[0] // height, one, 0)


def solve_kernel(core_ref, content_hbm, mine_hbm, other_hbm, parts_hbm, select_hbm, factor_hbm, kept_hbm, out_hbm,
                 content, low, parts, coef, factor, kept, state, out, sems, out_sems):
    core = core_ref[0]
    height = out.shape[0] // BLOCKS
    copies = [
        pltpu.make_async_copy(src, dst, sems.at[i])
        for i, (src, dst) in enumerate((
            (content_hbm, content),
            (parts_hbm, parts),
            (mine_hbm, low.at[core]),
            (other_hbm, low.at[1 - core]),
            (select_hbm, coef),
            (factor_hbm, factor),
            (kept_hbm, kept),
        ))
    ]
    for copy in copies:
        copy.start()
    for copy in copies[:2]:
        copy.wait()
    each = CHUNK
    for k in range(STEPS):
        x = content[:, k * NB:(k + 1) * NB, :].reshape(2 * NB, -1).astype(F32)
        if k == 1:
            for copy in copies[2:5]:
                copy.wait()
        if k:
            for j in range(k):
                at = start_of(k) + 2 * NB * j + NB
                for side in range(2):
                    for r in range(0, NB, each):
                        row = (2 * PAIRS.index((k, j)) + 1 - side) * NB + r
                        held, inside = divmod(row // each, low.shape[1])
                        here = side * NB + r
                        coef[here:here + each, at:at + NB] = coef[here:here + each, at:at + NB] * low[held, inside]
            at = start_of(k)
            x = x + jnp.dot(coef[:, at:at + 2 * NB * k], state[:2 * NB * k, :], preferred_element_type=F32)
        y = x.astype(BF)
        state[2 * NB * k:2 * NB * k + NB, :] = y[:NB]
        u = jnp.dot(parts[k], y[NB:], preferred_element_type=F32)
        state[2 * NB * k + NB:2 * NB * (k + 1), :] = (u[:NB] + (u[NB:2 * NB] + u[2 * NB:])).astype(BF)
    for copy in copies[5:]:
        copy.wait()
    writes = []
    for b in range(BLOCKS):
        at = b * height
        new = jnp.dot(factor[at:at + height, :], state[...], preferred_element_type=F32)
        out[at:at + height, :] = (kept[at:at + height, :].astype(F32) + new).astype(BF)
        writes.append(pltpu.make_async_copy(out.at[at:at + height], out_hbm.at[at:at + height], out_sems.at[b]))
        writes[-1].start()
    for write in writes:
        write.wait()


def cost(flops, nbytes):
    return pl.CostEstimate(flops=flops, bytes_accessed=nbytes, transcendentals=0)


def spread(x, axes, parts):
    return lax.all_to_all(jnp.broadcast_to(x[None], (parts,) + x.shape), axes, 0, 0, tiled=True)


def per_device(ny, nz, nx, nc, matrix, panels, inverses, pivots):
    nzx = nz * nx
    local, width = matrix.shape
    held = panels.shape[1]
    y, core = lax.axis_index("y"), lax.axis_index("c")
    zx = lax.axis_index(("z", "x"))
    first = y * local
    swap = [(0, 1), (1, 0)]
    first1 = first.reshape(1).astype(jnp.int32)
    core1 = core.reshape(1).astype(jnp.int32)

    share = pl.pallas_call(
        share_kernel,
        out_shape=jax.ShapeDtypeStruct((2, TOP, width), BF),
        in_specs=[SM, VM, VM],
        out_specs=VM,
        scratch_shapes=[pltpu.VMEM((TOP, local), BF)],
        cost_estimate=cost(2 * TOP * local * width, 4 << 20),
    )(first1, pivots, matrix)
    content = lax.psum(share, "y")
    panels, pivots, _ = lax.optimization_barrier((panels, pivots, share))

    def gather(panels, pivots):
        mine = spread(panels.reshape(STEPS * held, NB), "z", nz)
        mine = spread(mine, "x", nx)

        idx = []
        for k, j in PAIRS:
            for rows in (pivots[k], k * NB + jnp.arange(NB, dtype=jnp.int32)):
                here = rows - first
                pb = here // held
                at = ((pb // nc % nx * nz + pb // nc // nx) * STEPS + j) * held + here % held
                idx.append(jnp.where((here >= 0) & (here < local) & (pb % nc == core), at, -1))
        chunk = -(-len(idx) * NB // (nzx * nc) // CHUNK) * CHUNK
        idx = jnp.concatenate(idx + [jnp.full((chunk * nzx * nc - len(idx) * NB,), -1, jnp.int32)])
        idx = lax.dynamic_slice(idx.reshape(nc, nzx, chunk), (0, zx, 0), (nc, 1, chunk)).reshape(nc * chunk)
        part = jnp.take(mine.reshape(-1, NB), jnp.maximum(idx, 0), axis=0)
        part = jnp.where((idx >= 0)[:, None], part, jnp.zeros((), BF)).reshape(1, nc, chunk, NB)
        part = jnp.broadcast_to(part, (ny, nc, chunk, NB)).reshape(ny * nc, chunk, NB)
        part = lax.all_to_all(part, ("y", "c"), 0, 0, tiled=True).astype(F32).sum(0).astype(BF)

        part, mine = lax.optimization_barrier((part, mine))
        other = lax.ppermute(mine, "c", swap)
        low_mine = spread(part, ("z", "x"), nzx)

        both = [a.reshape(nx, nz, STEPS, held, NB) for a in (mine, other)]
        both = jnp.stack([jnp.where(core == 0, both[0], both[1]), jnp.where(core == 0, both[1], both[0])])
        full = both.transpose(3, 2, 1, 0, 4, 5).reshape(STEPS, local, NB)
        factor, kept, select, parts = pl.pallas_call(
            rows_kernel,
            out_shape=(
                jax.ShapeDtypeStruct((local, 2 * TOP), BF),
                jax.ShapeDtypeStruct((local, width), BF),
                jax.ShapeDtypeStruct((2 * NB, start_of(STEPS)), BF),
                jax.ShapeDtypeStruct((STEPS, 3 * NB, NB), BF),
            ),
            in_specs=[SM, VM, VM, VM, VM],
            out_specs=(VM, VM, VM, VM),
            cost_estimate=cost(2 * TOP * local * NB, 12 << 20),
        )(first1, pivots, full, matrix, inverses)
        low_mine, factor, kept, select, parts = lax.optimization_barrier((low_mine, factor, kept, select, parts))
        return low_mine, lax.ppermute(low_mine, "c", swap), factor, kept, select, parts

    def nothing(panels, pivots):
        return tuple(jnp.zeros(o.shape, o.dtype) for o in jax.eval_shape(gather, panels, pivots))

    low_mine, low_other, factor, kept, select, parts = lax.cond(y < ny, gather, nothing, panels, pivots)

    chunk = low_mine.size // (nzx * NB)
    low_shape = (nzx * chunk // CHUNK, CHUNK, NB)
    return pl.pallas_call(
        solve_kernel,
        out_shape=jax.ShapeDtypeStruct((local, width), BF),
        in_specs=[SM] + [ANY] * 7,
        out_specs=ANY,
        scratch_shapes=[
            pltpu.VMEM((2, TOP, width), BF),
            pltpu.VMEM((2,) + low_shape, BF),
            pltpu.VMEM(parts.shape, BF),
            pltpu.VMEM(select.shape, BF),
            pltpu.VMEM(factor.shape, BF),
            pltpu.VMEM((local, width), BF),
            pltpu.VMEM((2 * TOP, width), BF),
            pltpu.VMEM((local, width), BF),
            pltpu.SemaphoreType.DMA((7,)),
            pltpu.SemaphoreType.DMA((BLOCKS,)),
        ],
        cost_estimate=cost(4 * TOP * local * width, 16 << 20),
    )(core1, content, low_mine.reshape(low_shape), low_other.reshape(low_shape), parts, select, factor, kept)


def solution(mesh):
    ny, npb = mesh.devices.shape
    nz, nx, nc = (8, 4, 2) if npb == 64 else (1, npb // 2, 2)
    fine = Mesh(mesh.devices.reshape(ny, nz, nx, nc), ("y", "z", "x", "c"))
    cols = ("z", "x", "c")
    in_specs = (P("y", cols), P(None, ("y",) + cols, None), P(), P())
    return jax.shard_map(
        functools.partial(per_device, ny, nz, nx, nc), mesh=fine, in_specs=in_specs, out_specs=P("y", cols), check_vma=False
    )
```

```python
import functools

import jax
import jax.numpy as jnp
from jax import lax
from jax.experimental import pallas as pl
from jax.experimental.pallas import tpu as pltpu
from jax.sharding import Mesh
from jax.sharding import PartitionSpec as P

NB = 128
STEPS = 6
TOP = NB * STEPS
PAIRS = [(k, j) for k in range(1, STEPS) for j in range(k)]
CHUNK = 64
BLOCKS = 3
BF = jnp.bfloat16
F32 = jnp.float32
VM = pl.BlockSpec(memory_space=pltpu.VMEM)
SM = pl.BlockSpec(memory_space=pltpu.SMEM)
ANY = pl.BlockSpec(memory_space=pl.ANY)


def start_of(k):
    return 2 * NB * (k * (k - 1) // 2)


def iota(shape, dim):
    return lax.broadcasted_iota(jnp.int32, shape, dim)


def columns(row):
    return jnp.broadcast_to(row.astype(F32), (NB, NB)).T.astype(jnp.int32)


def masks(k, rows_ref):
    ones = jnp.ones((NB, NB), BF)
    ids = jnp.concatenate([iota((NB, NB), 0) + k * NB, columns(rows_ref[k:k + 1, :])])
    found = jnp.zeros((2 * NB, NB), F32)
    out = []
    for j in reversed(range(k)):
        same = jnp.where(ids == rows_ref[j:j + 1, :], 1.0, 0.0).astype(F32)
        live = 1.0 - found
        out.append((j, same * live, live))
        hit = jnp.dot(same.astype(BF), ones, preferred_element_type=F32)
        found = jnp.maximum(found, hit)
    return ids, out, found < 0.5


def share_kernel(first_ref, rows_ref, matrix_hbm, share_hbm, matrix, hot, share, sems):
    load = pltpu.make_async_copy(matrix_hbm, matrix, sems.at[0])
    load.start()
    first = first_ref[0]
    local, width = matrix.shape
    fresh = []
    for k in range(STEPS):
        ids, _, new = masks(k, rows_ref)
        fresh.append(new)
        at = k * NB
        where = ids[NB:] - first
        for c in range(0, local, NB):
            hot[at:at + NB, c:c + NB] = jnp.where(iota((NB, NB), 1) + c == where, 1.0, 0.0).astype(BF)
    load.wait()
    for k in range(STEPS):
        at = k * NB
        for c in range(0, width, NB):
            top = matrix[at:at + NB, c:c + NB].astype(F32)
            share[0, at:at + NB, c:c + NB] = jnp.where(fresh[k][:NB] & (first == 0), top, 0.0).astype(BF)
    stores = [pltpu.make_async_copy(share.at[0], share_hbm.at[0], sems.at[0])]
    stores[0].start()
    for k in range(0, STEPS, 2):
        at = k * NB
        row = jnp.dot(hot[at:at + 2 * NB, :], matrix[...], preferred_element_type=F32)
        for i in range(2):
            for c in range(0, width, NB):
                here = slice(at + i * NB, at + (i + 1) * NB)
                new = jnp.where(fresh[k + i][NB:], row[i * NB:(i + 1) * NB, c:c + NB], 0.0)
                share[1, here, c:c + NB] = new.astype(BF)
        both = pl.ds(at, 2 * NB)
        stores.append(pltpu.make_async_copy(share.at[1, both], share_hbm.at[1, both], sems.at[1 + k // 2]))
        stores[-1].start()
    for store in stores:
        store.wait()


def rows_kernel(first_ref, rows_ref, panels_ref, matrix_ref, factor_ref, kept_ref, select_ref):
    for k in range(1, STEPS):
        for j, same, live in masks(k, rows_ref)[1]:
            at = start_of(k) + 2 * NB * j
            select_ref[:, at:at + NB] = same.astype(BF)
            select_ref[:, at + NB:at + 2 * NB] = (-live).astype(BF)
    ones = jnp.ones((NB, NB), BF)
    height = 2 * NB

    def one(step, carry):
        at = pl.multiple_of(step * height, height)
        ids = iota((height, NB), 0) + first_ref[0] + at
        is_top = ids < TOP
        found = jnp.zeros((height, NB), F32)
        for j in reversed(range(STEPS)):
            same = jnp.where((ids == rows_ref[j:j + 1, :]) & ~is_top, 1.0, 0.0).astype(F32)
            live = 1.0 - found
            factor_ref[pl.ds(at, height), 2 * NB * j:2 * NB * j + NB] = (same * live).astype(BF)
            diag = jnp.where(ids - NB * j == iota((height, NB), 1), 1.0, 0.0).astype(F32)
            lower = -live * panels_ref[j, pl.ds(at, height), :].astype(F32)
            factor_ref[pl.ds(at, height), 2 * NB * j + NB:2 * NB * (j + 1)] = jnp.where(is_top, diag, lower).astype(BF)
            hit = jnp.dot(same.astype(BF), ones, preferred_element_type=F32)
            found = jnp.maximum(found, hit)
        fresh = (found < 0.5) & ~is_top
        for c in range(0, matrix_ref.shape[1], NB):
            old = matrix_ref[pl.ds(at, height), c:c + NB].astype(F32)
            kept_ref[pl.ds(at, height), c:c + NB] = jnp.where(fresh, old, 0.0).astype(BF)
        return carry

    lax.fori_loop(0, matrix_ref.shape[0] // height, one, 0)


def solve_kernel(core_ref, content_hbm, mine_hbm, other_hbm, inverses_hbm, select_hbm, factor_hbm, kept_hbm, out_hbm,
                 content, low, inverses, parts, coef, factor, kept, state, out, sems, out_sems):
    core = core_ref[0]
    height = out.shape[0] // BLOCKS
    copies = [
        pltpu.make_async_copy(src, dst, sems.at[i])
        for i, (src, dst) in enumerate((
            (inverses_hbm, inverses),
            (content_hbm, content),
            (mine_hbm, low.at[core]),
            (other_hbm, low.at[1 - core]),
            (select_hbm, coef),
            (factor_hbm, factor),
            (kept_hbm, kept),
        ))
    ]
    for copy in copies:
        copy.start()
    copies[0].wait()
    for k in range(STEPS):
        rest = inverses[k]
        for i in range(3):
            parts[k, i * NB:(i + 1) * NB, :] = rest.astype(BF)
            rest = rest - rest.astype(BF).astype(F32)
    copies[1].wait()
    each = CHUNK
    for k in range(STEPS):
        x = content[:, k * NB:(k + 1) * NB, :].reshape(2 * NB, -1).astype(F32)
        if k == 1:
            for copy in copies[2:5]:
                copy.wait()
        if k:
            for j in range(k):
                at = start_of(k) + 2 * NB * j + NB
                for side in range(2):
                    for r in range(0, NB, each):
                        row = (2 * PAIRS.index((k, j)) + 1 - side) * NB + r
                        held, inside = divmod(row // each, low.shape[1])
                        here = side * NB + r
                        coef[here:here + each, at:at + NB] = coef[here:here + each, at:at + NB] * low[held, inside]
            at = start_of(k)
            x = x + jnp.dot(coef[:, at:at + 2 * NB * k], state[:2 * NB * k, :], preferred_element_type=F32)
        y = x.astype(BF)
        state[2 * NB * k:2 * NB * k + NB, :] = y[:NB]
        u = jnp.dot(parts[k], y[NB:], preferred_element_type=F32)
        state[2 * NB * k + NB:2 * NB * (k + 1), :] = (u[:NB] + (u[NB:2 * NB] + u[2 * NB:])).astype(BF)
    for copy in copies[5:]:
        copy.wait()
    writes = []
    for b in range(BLOCKS):
        at = b * height
        new = jnp.dot(factor[at:at + height, :], state[...], preferred_element_type=F32)
        out[at:at + height, :] = (kept[at:at + height, :].astype(F32) + new).astype(BF)
        writes.append(pltpu.make_async_copy(out.at[at:at + height], out_hbm.at[at:at + height], out_sems.at[b]))
        writes[-1].start()
    for write in writes:
        write.wait()


def cost(flops, nbytes):
    return pl.CostEstimate(flops=flops, bytes_accessed=nbytes, transcendentals=0)


def spread(x, axes, parts):
    return lax.all_to_all(jnp.broadcast_to(x[None], (parts,) + x.shape), axes, 0, 0, tiled=True)


def per_device(ny, nz, nx, nc, matrix, panels, inverses, pivots):
    nzx = nz * nx
    local, width = matrix.shape
    held = panels.shape[1]
    y, core = lax.axis_index("y"), lax.axis_index("c")
    z, x = lax.axis_index("z"), lax.axis_index("x")
    first = y * local
    swap = [(0, 1), (1, 0)]
    first1 = first.reshape(1).astype(jnp.int32)
    core1 = core.reshape(1).astype(jnp.int32)

    column = jnp.broadcast_to(panels.reshape(1, STEPS * held, NB), (nz, STEPS * held, NB))

    share = pl.pallas_call(
        share_kernel,
        out_shape=jax.ShapeDtypeStruct((2, TOP, width), BF),
        in_specs=[SM, VM, ANY],
        out_specs=ANY,
        scratch_shapes=[
            pltpu.VMEM((local, width), BF),
            pltpu.VMEM((TOP, local), BF),
            pltpu.VMEM((2, TOP, width), BF),
            pltpu.SemaphoreType.DMA((4,)),
        ],
        cost_estimate=cost(2 * TOP * local * width, 4 << 20),
    )(first1, pivots, matrix)
    content = lax.psum(share, "y")
    column, pivots, _ = lax.optimization_barrier((column, pivots, share))

    def gather(column, pivots):
        column = lax.all_to_all(column, "z", 0, 0, tiled=True)

        idx = []
        for k, j in PAIRS:
            for rows in (pivots[k], k * NB + jnp.arange(NB, dtype=jnp.int32)):
                here = rows - first
                pb = here // held
                at = (pb // (nx * nc) * STEPS + j) * held + here % held
                owned = (here >= 0) & (here < local) & (pb % (nx * nc) == x * nc + core)
                idx.append(jnp.where(owned, at, -1))
        chunk = -(-len(idx) * NB // (nzx * nc) // CHUNK) * CHUNK
        idx = jnp.concatenate(idx + [jnp.full((chunk * nzx * nc - len(idx) * NB,), -1, jnp.int32)])
        idx = lax.dynamic_slice(idx.reshape(nc, nz, nx * chunk), (0, z, 0), (nc, 1, nx * chunk)).reshape(nc * nx * chunk)
        part = jnp.take(column.reshape(-1, NB), jnp.maximum(idx, 0), axis=0)
        part = jnp.where((idx >= 0)[:, None], part, jnp.zeros((), BF)).reshape(nc * nx, chunk, NB)
        part = lax.all_to_all(part, ("c", "x"), 0, 0, tiled=True).astype(F32).sum(0).astype(BF)
        part = spread(part, "y", ny).reshape(ny, chunk, NB).astype(F32).sum(0).astype(BF)

        blocks = [column] + [lax.ppermute(column, "x", [((i + s) % nx, i) for i in range(nx)]) for s in range(1, nx)]
        mine = lax.dynamic_slice_in_dim(jnp.stack(blocks + blocks), (nx - x) % nx, nx)
        part, mine = lax.optimization_barrier((part, mine))
        other = lax.ppermute(mine, "c", swap)
        low_mine = spread(part, ("z", "x"), nzx)

        both = [a.reshape(nx, nz, STEPS, held, NB) for a in (mine, other)]
        both = jnp.stack([jnp.where(core == 0, both[0], both[1]), jnp.where(core == 0, both[1], both[0])])
        full = both.transpose(3, 2, 1, 0, 4, 5).reshape(STEPS, local, NB)
        factor, kept, select = pl.pallas_call(
            rows_kernel,
            out_shape=(
                jax.ShapeDtypeStruct((local, 2 * TOP), BF),
                jax.ShapeDtypeStruct((local, width), BF),
                jax.ShapeDtypeStruct((2 * NB, start_of(STEPS)), BF),
            ),
            in_specs=[SM, VM, VM, VM],
            out_specs=(VM, VM, VM),
            cost_estimate=cost(2 * TOP * local * NB, 12 << 20),
        )(first1, pivots, full, matrix)
        low_mine, factor, kept, select = lax.optimization_barrier((low_mine, factor, kept, select))
        return low_mine, lax.ppermute(low_mine, "c", swap), factor, kept, select

    def nothing(column, pivots):
        return tuple(jnp.zeros(o.shape, o.dtype) for o in jax.eval_shape(gather, column, pivots))

    low_mine, low_other, factor, kept, select = lax.cond(y < ny, gather, nothing, column, pivots)

    chunk = low_mine.size // (nzx * NB)
    low_shape = (nzx * chunk // CHUNK, CHUNK, NB)
    return pl.pallas_call(
        solve_kernel,
        out_shape=jax.ShapeDtypeStruct((local, width), BF),
        in_specs=[SM] + [ANY] * 7,
        out_specs=ANY,
        scratch_shapes=[
            pltpu.VMEM((2, TOP, width), BF),
            pltpu.VMEM((2,) + low_shape, BF),
            pltpu.VMEM(inverses.shape, F32),
            pltpu.VMEM((STEPS, 3 * NB, NB), BF),
            pltpu.VMEM(select.shape, BF),
            pltpu.VMEM(factor.shape, BF),
            pltpu.VMEM((local, width), BF),
            pltpu.VMEM((2 * TOP, width), BF),
            pltpu.VMEM((local, width), BF),
            pltpu.SemaphoreType.DMA((7,)),
            pltpu.SemaphoreType.DMA((BLOCKS,)),
        ],
        cost_estimate=cost(4 * TOP * local * width, 16 << 20),
    )(core1, content, low_mine.reshape(low_shape), low_other.reshape(low_shape), inverses, select, factor, kept)


def solution(mesh):
    ny, npb = mesh.devices.shape
    nz, nx, nc = (8, 4, 2) if npb == 64 else (1, npb // 2, 2)
    fine = Mesh(mesh.devices.reshape(ny, nz, nx, nc), ("y", "z", "x", "c"))
    cols = ("z", "x", "c")
    in_specs = (P("y", cols), P(None, ("y",) + cols, None), P(), P())
    return jax.shard_map(
        functools.partial(per_device, ny, nz, nx, nc), mesh=fine, in_specs=in_specs, out_specs=P("y", cols), check_vma=False
    )
```

```python
import functools

import jax
import jax.numpy as jnp
from jax import lax
from jax.experimental import pallas as pl
from jax.experimental.pallas import tpu as pltpu
from jax.sharding import Mesh
from jax.sharding import PartitionSpec as P

NB = 128
STEPS = 6
TOP = NB * STEPS
PAIRS = [(k, j) for k in range(1, STEPS) for j in range(k)]
CHUNK = 64
BLOCKS = 3
LONG = 1 << 36
BF = jnp.bfloat16
F32 = jnp.float32
VM = pl.BlockSpec(memory_space=pltpu.VMEM)
SM = pl.BlockSpec(memory_space=pltpu.SMEM)
ANY = pl.BlockSpec(memory_space=pl.ANY)


def start_of(k):
    return 2 * NB * (k * (k - 1) // 2)


def iota(shape, dim):
    return lax.broadcasted_iota(jnp.int32, shape, dim)


def columns(row):
    return jnp.broadcast_to(row.astype(F32), (NB, NB)).T.astype(jnp.int32)


def matches(k, rows_ref):
    ids = jnp.concatenate([iota((NB, NB), 0) + k * NB, columns(rows_ref[k:k + 1, :])])
    return ids, [jnp.where(ids == rows_ref[j:j + 1, :], 1.0, 0.0).astype(F32) for j in range(k)]


def any_lane(same):
    return jnp.dot(same.astype(BF), jnp.ones((NB, NB), BF), preferred_element_type=F32)


def last_match(same):
    hits = [any_lane(s) for s in same]
    found = jnp.zeros(same[0].shape, F32)
    out = []
    for s, hit in zip(reversed(same), reversed(hits)):
        live = 1.0 - found
        out.append((s * live, live))
        found = jnp.maximum(found, hit)
    return out[::-1], found < 0.5


def share_kernel(first_ref, rows_ref, matrix_hbm, share_hbm, matrix, hot, share, sems):
    load = pltpu.make_async_copy(matrix_hbm, matrix, sems.at[0])
    load.start()
    first = first_ref[0]
    local, width = matrix.shape
    fresh = []
    for k in range(STEPS):
        ids, same = matches(k, rows_ref)
        fresh.append(any_lane(sum(same, jnp.zeros((2 * NB, NB), F32))) < 0.5)
        at = k * NB
        where = ids[NB:] - first
        for c in range(0, local, NB):
            hot[at:at + NB, c:c + NB] = jnp.where(iota((NB, NB), 1) + c == where, 1.0, 0.0).astype(BF)
    load.wait()
    for k in range(STEPS):
        at = k * NB
        for c in range(0, width, NB):
            top = matrix[at:at + NB, c:c + NB].astype(F32)
            share[0, at:at + NB, c:c + NB] = jnp.where(fresh[k][:NB] & (first == 0), top, 0.0).astype(BF)
    stores = [pltpu.make_async_copy(share.at[0], share_hbm.at[0], sems.at[0])]
    stores[0].start()
    for k in range(0, STEPS, 2):
        at = k * NB
        row = jnp.dot(hot[at:at + 2 * NB, :], matrix[...], preferred_element_type=F32)
        for i in range(2):
            for c in range(0, width, NB):
                here = slice(at + i * NB, at + (i + 1) * NB)
                new = jnp.where(fresh[k + i][NB:], row[i * NB:(i + 1) * NB, c:c + NB], 0.0)
                share[1, here, c:c + NB] = new.astype(BF)
        both = pl.ds(at, 2 * NB)
        stores.append(pltpu.make_async_copy(share.at[1, both], share_hbm.at[1, both], sems.at[1 + k // 2]))
        stores[-1].start()
    for store in stores:
        store.wait()


def select_kernel(rows_ref, select_ref):
    for k in range(1, STEPS):
        for j, (last, live) in enumerate(last_match(matches(k, rows_ref)[1])[0]):
            at = start_of(k) + 2 * NB * j
            select_ref[:, at:at + NB] = last.astype(BF)
            select_ref[:, at + NB:at + 2 * NB] = (-live).astype(BF)


def mark_kernel(first_ref, rows_ref, matrix_ref, last_ref, live_ref, kept_ref):
    height = 2 * NB

    def one(step, carry):
        at = pl.multiple_of(step * height, height)
        ids = iota((height, NB), 0) + first_ref[0] + at
        is_top = ids < TOP
        same = [jnp.where((ids == rows_ref[j:j + 1, :]) & ~is_top, 1.0, 0.0).astype(F32) for j in range(STEPS)]
        state, fresh = last_match(same)
        for j, (last, live) in enumerate(state):
            last_ref[pl.ds(at, height), NB * j:NB * (j + 1)] = last.astype(BF)
            live_ref[pl.ds(at, height), NB * j:NB * (j + 1)] = jnp.where(is_top, 0.0, -live).astype(BF)
        fresh = fresh & ~is_top
        for c in range(0, matrix_ref.shape[1], NB):
            old = matrix_ref[pl.ds(at, height), c:c + NB].astype(F32)
            kept_ref[pl.ds(at, height), c:c + NB] = jnp.where(fresh, old, 0.0).astype(BF)
        return carry

    lax.fori_loop(0, matrix_ref.shape[0] // height, one, 0)


def rows_kernel(first_ref, panels_ref, last_ref, live_ref, factor_ref):
    height = 2 * NB

    def one(step, carry):
        at = pl.multiple_of(step * height, height)
        block = pl.ds(at, height)
        ids = iota((height, NB), 0) + first_ref[0] + at
        for j in range(STEPS):
            here = 2 * NB * j
            factor_ref[block, here:here + NB] = last_ref[block, NB * j:NB * (j + 1)]
            diag = jnp.where((ids - NB * j == iota((height, NB), 1)) & (ids < TOP), 1.0, 0.0).astype(BF)
            lower = live_ref[block, NB * j:NB * (j + 1)] * panels_ref[j, block, :]
            factor_ref[block, here + NB:here + 2 * NB] = lower + diag
        return carry

    lax.fori_loop(0, panels_ref.shape[1] // height, one, 0)


def solve_kernel(core_ref, content_hbm, mine_hbm, other_hbm, inverses_hbm, select_hbm, factor_hbm, kept_hbm, out_hbm,
                 content, low, inverses, parts, coef, factor, kept, state, out, sems, out_sems):
    core = core_ref[0]
    height = out.shape[0] // BLOCKS
    copies = [
        pltpu.make_async_copy(src, dst, sems.at[i])
        for i, (src, dst) in enumerate((
            (inverses_hbm, inverses),
            (content_hbm, content),
            (mine_hbm, low.at[core]),
            (other_hbm, low.at[1 - core]),
            (select_hbm, coef),
            (factor_hbm, factor),
            (kept_hbm, kept),
        ))
    ]
    for copy in copies:
        copy.start()
    copies[0].wait()
    for k in range(STEPS):
        rest = inverses[k]
        for i in range(3):
            parts[k, i * NB:(i + 1) * NB, :] = rest.astype(BF)
            rest = rest - rest.astype(BF).astype(F32)
    copies[1].wait()
    each = CHUNK
    for k in range(STEPS):
        x = content[:, k * NB:(k + 1) * NB, :].reshape(2 * NB, -1).astype(F32)
        if k == 1:
            for copy in copies[2:5]:
                copy.wait()
        if k:
            for j in range(k):
                at = start_of(k) + 2 * NB * j + NB
                for side in range(2):
                    for r in range(0, NB, each):
                        row = (2 * PAIRS.index((k, j)) + 1 - side) * NB + r
                        held, inside = divmod(row // each, low.shape[1])
                        here = side * NB + r
                        coef[here:here + each, at:at + NB] = coef[here:here + each, at:at + NB] * low[held, inside]
            at = start_of(k)
            x = x + jnp.dot(coef[:, at:at + 2 * NB * k], state[:2 * NB * k, :], preferred_element_type=F32)
        y = x.astype(BF)
        state[2 * NB * k:2 * NB * k + NB, :] = y[:NB]
        u = jnp.dot(parts[k], y[NB:], preferred_element_type=F32)
        state[2 * NB * k + NB:2 * NB * (k + 1), :] = (u[:NB] + (u[NB:2 * NB] + u[2 * NB:])).astype(BF)
    for copy in copies[5:]:
        copy.wait()
    writes = []
    for b in range(BLOCKS):
        at = b * height
        new = jnp.dot(factor[at:at + height, :], state[...], preferred_element_type=F32)
        out[at:at + height, :] = (kept[at:at + height, :].astype(F32) + new).astype(BF)
        writes.append(pltpu.make_async_copy(out.at[at:at + height], out_hbm.at[at:at + height], out_sems.at[b]))
        writes[-1].start()
    for write in writes:
        write.wait()


def cost(flops, nbytes):
    return pl.CostEstimate(flops=flops, bytes_accessed=nbytes, transcendentals=0)


def spread(x, axes, parts):
    return lax.all_to_all(jnp.broadcast_to(x[None], (parts,) + x.shape), axes, 0, 0, tiled=True)


def per_device(ny, nz, nx, nc, matrix, panels, inverses, pivots):
    nzx = nz * nx
    local, width = matrix.shape
    held = panels.shape[1]
    y, core = lax.axis_index("y"), lax.axis_index("c")
    z, x = lax.axis_index("z"), lax.axis_index("x")
    first = y * local
    swap = [(0, 1), (1, 0)]
    first1 = first.reshape(1).astype(jnp.int32)
    core1 = core.reshape(1).astype(jnp.int32)

    share = pl.pallas_call(
        share_kernel,
        out_shape=jax.ShapeDtypeStruct((2, TOP, width), BF),
        in_specs=[SM, VM, ANY],
        out_specs=ANY,
        scratch_shapes=[
            pltpu.VMEM((local, width), BF),
            pltpu.VMEM((TOP, local), BF),
            pltpu.VMEM((2, TOP, width), BF),
            pltpu.SemaphoreType.DMA((4,)),
        ],
        cost_estimate=cost(2 * TOP * local * width, 4 << 20),
    )(first1, pivots, matrix)
    content = lax.psum(share, "y")
    panels, pivots, _ = lax.optimization_barrier((panels, pivots, share))

    def gather(panels, pivots):
        column = spread(panels.reshape(STEPS * held, NB), "z", nz).reshape(nz, STEPS * held, NB)

        idx = []
        for k, j in PAIRS:
            for rows in (pivots[k], k * NB + jnp.arange(NB, dtype=jnp.int32)):
                here = rows - first
                pb = here // held
                at = (pb // (nx * nc) * STEPS + j) * held + here % held
                owned = (here >= 0) & (here < local) & (pb % (nx * nc) == x * nc + core)
                idx.append(jnp.where(owned, at, -1))
        chunk = -(-len(idx) * NB // (nzx * nc) // CHUNK) * CHUNK
        idx = jnp.concatenate(idx + [jnp.full((chunk * nzx * nc - len(idx) * NB,), -1, jnp.int32)])
        idx = lax.dynamic_slice(idx.reshape(nc, nz, nx * chunk), (0, z, 0), (nc, 1, nx * chunk)).reshape(nc * nx * chunk)
        part = jnp.take(column.reshape(-1, NB), jnp.maximum(idx, 0), axis=0)
        part = jnp.where((idx >= 0)[:, None], part, jnp.zeros((), BF)).reshape(nc * nx, chunk, NB)
        part = lax.all_to_all(part, ("c", "x"), 0, 0, tiled=True)
        part = part.astype(F32).sum(0).astype(BF)
        part = spread(part, "y", ny).reshape(ny, chunk, NB).astype(F32).sum(0).astype(BF)

        blocks = [column] + [lax.ppermute(column, "x", [((i + s) % nx, i) for i in range(nx)]) for s in range(1, nx)]
        mine = lax.dynamic_slice_in_dim(jnp.stack(blocks + blocks), (nx - x) % nx, nx)
        part = jnp.broadcast_to(part[None], (nzx, chunk, NB))
        part, mine, pivots = lax.optimization_barrier((part, mine, pivots))
        other = lax.ppermute(mine, "c", swap)
        select = pl.pallas_call(
            select_kernel,
            out_shape=jax.ShapeDtypeStruct((2 * NB, start_of(STEPS)), BF),
            in_specs=[VM],
            out_specs=VM,
            cost_estimate=cost(LONG, 2 << 20),
        )(pivots)
        marked = pl.pallas_call(
            mark_kernel,
            out_shape=(jax.ShapeDtypeStruct((local, TOP), BF), jax.ShapeDtypeStruct((local, TOP), BF), jax.ShapeDtypeStruct((local, width), BF)),
            in_specs=[SM, VM, VM],
            out_specs=(VM, VM, VM),
            cost_estimate=cost(LONG, 6 << 20),
        )(first1, pivots, matrix)
        other, select, *marked = lax.optimization_barrier((other, select, *marked))
        low_mine = lax.all_to_all(part, ("z", "x"), 0, 0, tiled=True)

        both = [a.reshape(nx, nz, STEPS, held, NB) for a in (mine, other)]
        both = jnp.stack([jnp.where(core == 0, both[0], both[1]), jnp.where(core == 0, both[1], both[0])])
        full = both.transpose(3, 2, 1, 0, 4, 5).reshape(STEPS, local, NB)
        factor = pl.pallas_call(
            rows_kernel,
            out_shape=jax.ShapeDtypeStruct((local, 2 * TOP), BF),
            in_specs=[SM, VM, VM, VM],
            out_specs=VM,
            cost_estimate=cost(2 * TOP * local * NB, 12 << 20),
        )(first1, full, *marked[:2])
        kept = marked[2]
        low_mine, factor = lax.optimization_barrier((low_mine, factor))
        return low_mine, lax.ppermute(low_mine, "c", swap), factor, kept, select

    def nothing(panels, pivots):
        return tuple(jnp.zeros(o.shape, o.dtype) for o in jax.eval_shape(gather, panels, pivots))

    low_mine, low_other, factor, kept, select = lax.cond(y < ny, gather, nothing, panels, pivots)

    chunk = low_mine.size // (nzx * NB)
    low_shape = (nzx * chunk // CHUNK, CHUNK, NB)
    return pl.pallas_call(
        solve_kernel,
        out_shape=jax.ShapeDtypeStruct((local, width), BF),
        in_specs=[SM] + [ANY] * 7,
        out_specs=ANY,
        scratch_shapes=[
            pltpu.VMEM((2, TOP, width), BF),
            pltpu.VMEM((2,) + low_shape, BF),
            pltpu.VMEM(inverses.shape, F32),
            pltpu.VMEM((STEPS, 3 * NB, NB), BF),
            pltpu.VMEM(select.shape, BF),
            pltpu.VMEM(factor.shape, BF),
            pltpu.VMEM((local, width), BF),
            pltpu.VMEM((2 * TOP, width), BF),
            pltpu.VMEM((local, width), BF),
            pltpu.SemaphoreType.DMA((7,)),
            pltpu.SemaphoreType.DMA((BLOCKS,)),
        ],
        cost_estimate=cost(4 * TOP * local * width, 16 << 20),
    )(core1, content, low_mine.reshape(low_shape), low_other.reshape(low_shape), inverses, select, factor, kept)


def solution(mesh):
    ny, npb = mesh.devices.shape
    nz, nx, nc = (8, 4, 2) if npb == 64 else (1, npb // 2, 2)
    fine = Mesh(mesh.devices.reshape(ny, nz, nx, nc), ("y", "z", "x", "c"))
    cols = ("z", "x", "c")
    in_specs = (P("y", cols), P(None, ("y",) + cols, None), P(), P())
    return jax.shard_map(
        functools.partial(per_device, ny, nz, nx, nc), mesh=fine, in_specs=in_specs, out_specs=P("y", cols), check_vma=False
    )
```

```python
import functools

import jax
import jax.numpy as jnp
from jax import lax
from jax.experimental import pallas as pl
from jax.experimental.pallas import tpu as pltpu
from jax.sharding import Mesh
from jax.sharding import PartitionSpec as P

NB = 128
STEPS = 6
TOP = NB * STEPS
PAIRS = [(k, j) for k in range(1, STEPS) for j in range(k)]
CHUNK = 64
BLOCKS = 3
LONG = 1 << 36
BF = jnp.bfloat16
F32 = jnp.float32
VM = pl.BlockSpec(memory_space=pltpu.VMEM)
SM = pl.BlockSpec(memory_space=pltpu.SMEM)
ANY = pl.BlockSpec(memory_space=pl.ANY)


def start_of(k):
    return 2 * NB * (k * (k - 1) // 2)


def iota(shape, dim):
    return lax.broadcasted_iota(jnp.int32, shape, dim)


def columns(row):
    return jnp.broadcast_to(row.astype(F32), (NB, NB)).T.astype(jnp.int32)


def matches(k, rows_ref):
    ids = jnp.concatenate([iota((NB, NB), 0) + k * NB, columns(rows_ref[k:k + 1, :])])
    return ids, [jnp.where(ids == rows_ref[j:j + 1, :], 1.0, 0.0).astype(F32) for j in range(k)]


def any_lane(same):
    return jnp.dot(same.astype(BF), jnp.ones((NB, NB), BF), preferred_element_type=F32)


def last_match(same):
    hits = [any_lane(s) for s in same]
    found = jnp.zeros(same[0].shape, F32)
    out = []
    for s, hit in zip(reversed(same), reversed(hits)):
        live = 1.0 - found
        out.append((s * live, live))
        found = jnp.maximum(found, hit)
    return out[::-1], found < 0.5


def share_kernel(first_ref, rows_ref, matrix_hbm, share_hbm, matrix, hot, share, sems):
    load = pltpu.make_async_copy(matrix_hbm, matrix, sems.at[0])
    load.start()
    first = first_ref[0]
    local, width = matrix.shape
    fresh = []
    for k in range(STEPS):
        ids, same = matches(k, rows_ref)
        fresh.append(any_lane(sum(same, jnp.zeros((2 * NB, NB), F32))) < 0.5)
        at = k * NB
        where = ids[NB:] - first
        for c in range(0, local, NB):
            hot[at:at + NB, c:c + NB] = jnp.where(iota((NB, NB), 1) + c == where, 1.0, 0.0).astype(BF)
    load.wait()
    for k in range(STEPS):
        at = k * NB
        for c in range(0, width, NB):
            top = matrix[at:at + NB, c:c + NB].astype(F32)
            share[0, at:at + NB, c:c + NB] = jnp.where(fresh[k][:NB] & (first == 0), top, 0.0).astype(BF)
    stores = [pltpu.make_async_copy(share.at[0], share_hbm.at[0], sems.at[0])]
    stores[0].start()
    for k in range(0, STEPS, 2):
        at = k * NB
        row = jnp.dot(hot[at:at + 2 * NB, :], matrix[...], preferred_element_type=F32)
        for i in range(2):
            for c in range(0, width, NB):
                here = slice(at + i * NB, at + (i + 1) * NB)
                new = jnp.where(fresh[k + i][NB:], row[i * NB:(i + 1) * NB, c:c + NB], 0.0)
                share[1, here, c:c + NB] = new.astype(BF)
        both = pl.ds(at, 2 * NB)
        stores.append(pltpu.make_async_copy(share.at[1, both], share_hbm.at[1, both], sems.at[1 + k // 2]))
        stores[-1].start()
    for store in stores:
        store.wait()


def select_kernel(rows_ref, select_ref):
    for k in range(1, STEPS):
        for j, (last, live) in enumerate(last_match(matches(k, rows_ref)[1])[0]):
            at = start_of(k) + 2 * NB * j
            select_ref[:, at:at + NB] = last.astype(BF)
            select_ref[:, at + NB:at + 2 * NB] = (-live).astype(BF)


def mark_kernel(first_ref, rows_ref, matrix_ref, last_ref, live_ref, kept_ref):
    height = 2 * NB

    def one(step, carry):
        at = pl.multiple_of(step * height, height)
        ids = iota((height, NB), 0) + first_ref[0] + at
        is_top = ids < TOP
        same = [jnp.where((ids == rows_ref[j:j + 1, :]) & ~is_top, 1.0, 0.0).astype(F32) for j in range(STEPS)]
        state, fresh = last_match(same)
        for j, (last, live) in enumerate(state):
            last_ref[pl.ds(at, height), NB * j:NB * (j + 1)] = last.astype(BF)
            live_ref[pl.ds(at, height), NB * j:NB * (j + 1)] = jnp.where(is_top, 0.0, -live).astype(BF)
        fresh = fresh & ~is_top
        for c in range(0, matrix_ref.shape[1], NB):
            old = matrix_ref[pl.ds(at, height), c:c + NB].astype(F32)
            kept_ref[pl.ds(at, height), c:c + NB] = jnp.where(fresh, old, 0.0).astype(BF)
        return carry

    lax.fori_loop(0, matrix_ref.shape[0] // height, one, 0)


def rows_kernel(first_ref, panels_ref, live_ref, lower_ref):
    height = 2 * NB

    def one(step, carry):
        at = pl.multiple_of(step * height, height)
        block = pl.ds(at, height)
        ids = iota((height, NB), 0) + first_ref[0] + at
        for j in range(STEPS):
            here = slice(NB * j, NB * (j + 1))
            diag = jnp.where((ids - NB * j == iota((height, NB), 1)) & (ids < TOP), 1.0, 0.0).astype(BF)
            lower_ref[block, here] = live_ref[block, here] * panels_ref[j, block, :] + diag
        return carry

    lax.fori_loop(0, panels_ref.shape[1] // height, one, 0)


def solve_kernel(core_ref, content_hbm, mine_hbm, other_hbm, inverses_hbm, select_hbm, last_hbm, lower_hbm, kept_hbm, out_hbm,
                 content, low, inverses, parts, coef, last, lower, kept, state, moved, upper, out, sems, out_sems):
    core = core_ref[0]
    height = out.shape[0] // BLOCKS
    copies = [
        pltpu.make_async_copy(src, dst, sems.at[i])
        for i, (src, dst) in enumerate((
            (inverses_hbm, inverses),
            (content_hbm, content),
            (mine_hbm, low.at[core]),
            (other_hbm, low.at[1 - core]),
            (select_hbm, coef),
            (last_hbm, last),
            (lower_hbm, lower),
            (kept_hbm, kept),
        ))
    ]
    for copy in copies:
        copy.start()
    copies[0].wait()
    for k in range(STEPS):
        rest = inverses[k]
        for i in range(3):
            parts[k, i * NB:(i + 1) * NB, :] = rest.astype(BF)
            rest = rest - rest.astype(BF).astype(F32)
    copies[1].wait()
    each = CHUNK
    for k in range(STEPS):
        x = content[:, k * NB:(k + 1) * NB, :].reshape(2 * NB, -1).astype(F32)
        if k == 1:
            for copy in copies[2:5]:
                copy.wait()
        if k:
            for j in range(k):
                at = start_of(k) + 2 * NB * j + NB
                for side in range(2):
                    for r in range(0, NB, each):
                        row = (2 * PAIRS.index((k, j)) + 1 - side) * NB + r
                        held, inside = divmod(row // each, low.shape[1])
                        here = side * NB + r
                        coef[here:here + each, at:at + NB] = coef[here:here + each, at:at + NB] * low[held, inside]
            at = start_of(k)
            x = x + jnp.dot(coef[:, at:at + 2 * NB * k], state[:2 * NB * k, :], preferred_element_type=F32)
        y = x.astype(BF)
        state[2 * NB * k:2 * NB * k + NB, :] = y[:NB]
        moved[k * NB:(k + 1) * NB, :] = y[:NB]
        u = jnp.dot(parts[k], y[NB:], preferred_element_type=F32)
        u = (u[:NB] + (u[NB:2 * NB] + u[2 * NB:])).astype(BF)
        state[2 * NB * k + NB:2 * NB * (k + 1), :] = u
        upper[k * NB:(k + 1) * NB, :] = u
    for copy in copies[5:]:
        copy.wait()
    writes = []
    for b in range(BLOCKS):
        at = b * height
        new = jnp.dot(last[at:at + height, :], moved[...], preferred_element_type=F32)
        new = new + jnp.dot(lower[at:at + height, :], upper[...], preferred_element_type=F32)
        out[at:at + height, :] = (kept[at:at + height, :].astype(F32) + new).astype(BF)
        writes.append(pltpu.make_async_copy(out.at[at:at + height], out_hbm.at[at:at + height], out_sems.at[b]))
        writes[-1].start()
    for write in writes:
        write.wait()


def cost(flops, nbytes):
    return pl.CostEstimate(flops=flops, bytes_accessed=nbytes, transcendentals=0)


def spread(x, axes, parts):
    return lax.all_to_all(jnp.broadcast_to(x[None], (parts,) + x.shape), axes, 0, 0, tiled=True)


def per_device(ny, nz, nx, nc, matrix, panels, inverses, pivots):
    nzx = nz * nx
    local, width = matrix.shape
    held = panels.shape[1]
    y, core = lax.axis_index("y"), lax.axis_index("c")
    z, x = lax.axis_index("z"), lax.axis_index("x")
    first = y * local
    swap = [(0, 1), (1, 0)]
    first1 = first.reshape(1).astype(jnp.int32)
    core1 = core.reshape(1).astype(jnp.int32)

    share = pl.pallas_call(
        share_kernel,
        out_shape=jax.ShapeDtypeStruct((2, TOP, width), BF),
        in_specs=[SM, VM, ANY],
        out_specs=ANY,
        scratch_shapes=[
            pltpu.VMEM((local, width), BF),
            pltpu.VMEM((TOP, local), BF),
            pltpu.VMEM((2, TOP, width), BF),
            pltpu.SemaphoreType.DMA((4,)),
        ],
        cost_estimate=cost(2 * TOP * local * width, 4 << 20),
    )(first1, pivots, matrix)
    content = lax.psum(share, "y")
    panels, pivots, _ = lax.optimization_barrier((panels, pivots, share))

    def gather(panels, pivots):
        column = spread(panels.reshape(STEPS * held, NB), "z", nz).reshape(nz, STEPS * held, NB)

        idx = []
        for k, j in PAIRS:
            for rows in (pivots[k], k * NB + jnp.arange(NB, dtype=jnp.int32)):
                here = rows - first
                pb = here // held
                at = (pb // (nx * nc) * STEPS + j) * held + here % held
                owned = (here >= 0) & (here < local) & (pb % (nx * nc) == x * nc + core)
                idx.append(jnp.where(owned, at, -1))
        chunk = -(-len(idx) * NB // (nzx * nc) // CHUNK) * CHUNK
        idx = jnp.concatenate(idx + [jnp.full((chunk * nzx * nc - len(idx) * NB,), -1, jnp.int32)])
        idx = lax.dynamic_slice(idx.reshape(nc, nz, nx * chunk), (0, z, 0), (nc, 1, nx * chunk)).reshape(nc * nx * chunk)
        part = jnp.take(column.reshape(-1, NB), jnp.maximum(idx, 0), axis=0)
        part = jnp.where((idx >= 0)[:, None], part, jnp.zeros((), BF)).reshape(nc * nx, chunk, NB)
        part = lax.all_to_all(part, ("c", "x"), 0, 0, tiled=True)
        part = part.astype(F32).sum(0).astype(BF)
        part, pivots = lax.optimization_barrier((part, pivots))
        part = spread(part, "y", ny)
        marked = pl.pallas_call(
            mark_kernel,
            out_shape=(jax.ShapeDtypeStruct((local, TOP), BF), jax.ShapeDtypeStruct((local, TOP), BF), jax.ShapeDtypeStruct((local, width), BF)),
            in_specs=[SM, VM, VM],
            out_specs=(VM, VM, VM),
            cost_estimate=cost(4 * TOP * local * NB, 6 << 20),
        )(first1, pivots, matrix)
        part, *marked = lax.optimization_barrier((part, *marked))
        part = part.reshape(ny, chunk, NB).astype(F32).sum(0).astype(BF)

        blocks = [column] + [lax.ppermute(column, "x", [((i + s) % nx, i) for i in range(nx)]) for s in range(1, nx)]
        mine = lax.dynamic_slice_in_dim(jnp.stack(blocks + blocks), (nx - x) % nx, nx)
        part = jnp.broadcast_to(part[None], (nzx, chunk, NB))
        part, mine, pivots = lax.optimization_barrier((part, mine, pivots))
        other = lax.ppermute(mine, "c", swap)
        select = pl.pallas_call(
            select_kernel,
            out_shape=jax.ShapeDtypeStruct((2 * NB, start_of(STEPS)), BF),
            in_specs=[VM],
            out_specs=VM,
            cost_estimate=cost(LONG, 2 << 20),
        )(pivots)
        other, select = lax.optimization_barrier((other, select))
        low_mine = lax.all_to_all(part, ("z", "x"), 0, 0, tiled=True)

        both = [a.reshape(nx, nz, STEPS, held, NB) for a in (mine, other)]
        both = jnp.stack([jnp.where(core == 0, both[0], both[1]), jnp.where(core == 0, both[1], both[0])])
        full = both.transpose(3, 2, 1, 0, 4, 5).reshape(STEPS, local, NB)
        lower = pl.pallas_call(
            rows_kernel,
            out_shape=jax.ShapeDtypeStruct((local, TOP), BF),
            in_specs=[SM, VM, VM],
            out_specs=VM,
            cost_estimate=cost(2 * TOP * local * NB, 12 << 20),
        )(first1, full, marked[1])
        low_mine, lower = lax.optimization_barrier((low_mine, lower))
        return low_mine, lax.ppermute(low_mine, "c", swap), marked[0], lower, marked[2], select

    def nothing(panels, pivots):
        return tuple(jnp.zeros(o.shape, o.dtype) for o in jax.eval_shape(gather, panels, pivots))

    low_mine, low_other, last, lower, kept, select = lax.cond(y < ny, gather, nothing, panels, pivots)

    chunk = low_mine.size // (nzx * NB)
    low_shape = (nzx * chunk // CHUNK, CHUNK, NB)
    return pl.pallas_call(
        solve_kernel,
        out_shape=jax.ShapeDtypeStruct((local, width), BF),
        in_specs=[SM] + [ANY] * 8,
        out_specs=ANY,
        scratch_shapes=[
            pltpu.VMEM((2, TOP, width), BF),
            pltpu.VMEM((2,) + low_shape, BF),
            pltpu.VMEM(inverses.shape, F32),
            pltpu.VMEM((STEPS, 3 * NB, NB), BF),
            pltpu.VMEM(select.shape, BF),
            pltpu.VMEM(last.shape, BF),
            pltpu.VMEM(lower.shape, BF),
            pltpu.VMEM((local, width), BF),
            pltpu.VMEM((2 * TOP, width), BF),
            pltpu.VMEM((TOP, width), BF),
            pltpu.VMEM((TOP, width), BF),
            pltpu.VMEM((local, width), BF),
            pltpu.SemaphoreType.DMA((8,)),
            pltpu.SemaphoreType.DMA((BLOCKS,)),
        ],
        cost_estimate=cost(4 * TOP * local * width, 16 << 20),
    )(core1, content, low_mine.reshape(low_shape), low_other.reshape(low_shape), inverses, select, last, lower, kept)


def solution(mesh):
    ny, npb = mesh.devices.shape
    nz, nx, nc = (8, 4, 2) if npb == 64 else (1, npb // 2, 2)
    fine = Mesh(mesh.devices.reshape(ny, nz, nx, nc), ("y", "z", "x", "c"))
    cols = ("z", "x", "c")
    in_specs = (P("y", cols), P(None, ("y",) + cols, None), P(), P())
    return jax.shard_map(
        functools.partial(per_device, ny, nz, nx, nc), mesh=fine, in_specs=in_specs, out_specs=P("y", cols), check_vma=False
    )
```

```python
import functools

import jax
import jax.numpy as jnp
from jax import lax
from jax.experimental import pallas as pl
from jax.experimental.pallas import tpu as pltpu
from jax.sharding import Mesh
from jax.sharding import PartitionSpec as P

NB = 128
STEPS = 6
TOP = NB * STEPS
PAIRS = [(k, j) for k in range(1, STEPS) for j in range(k)]
CHUNK = 64
BLOCKS = 3
LONG = 1 << 36
BF = jnp.bfloat16
F32 = jnp.float32
VM = pl.BlockSpec(memory_space=pltpu.VMEM)
SM = pl.BlockSpec(memory_space=pltpu.SMEM)
ANY = pl.BlockSpec(memory_space=pl.ANY)


def start_of(k):
    return 2 * NB * (k * (k - 1) // 2)


def iota(shape, dim):
    return lax.broadcasted_iota(jnp.int32, shape, dim)


def columns(row):
    return jnp.broadcast_to(row.astype(F32), (NB, NB)).T.astype(jnp.int32)


def matches(k, rows_ref):
    ids = jnp.concatenate([iota((NB, NB), 0) + k * NB, columns(rows_ref[k:k + 1, :])])
    return ids, [jnp.where(ids == rows_ref[j:j + 1, :], 1.0, 0.0).astype(F32) for j in range(k)]


def any_lane(same):
    return jnp.dot(same.astype(BF), jnp.ones((NB, NB), BF), preferred_element_type=F32)


def last_match(same):
    hits = [any_lane(s) for s in same]
    found = jnp.zeros(same[0].shape, F32)
    out = []
    for s, hit in zip(reversed(same), reversed(hits)):
        live = 1.0 - found
        out.append((s * live, live))
        found = jnp.maximum(found, hit)
    return out[::-1], found < 0.5


def share_kernel(first_ref, rows_ref, matrix_hbm, share_hbm, matrix, hot, share, sems):
    load = pltpu.make_async_copy(matrix_hbm, matrix, sems.at[0])
    load.start()
    first = first_ref[0]
    local, width = matrix.shape
    fresh = []
    for k in range(STEPS):
        ids, same = matches(k, rows_ref)
        fresh.append(any_lane(sum(same, jnp.zeros((2 * NB, NB), F32))) < 0.5)
        at = k * NB
        where = ids[NB:] - first
        for c in range(0, local, NB):
            hot[at:at + NB, c:c + NB] = jnp.where(iota((NB, NB), 1) + c == where, 1.0, 0.0).astype(BF)
    load.wait()
    for k in range(STEPS):
        at = k * NB
        for c in range(0, width, NB):
            top = matrix[at:at + NB, c:c + NB].astype(F32)
            share[0, at:at + NB, c:c + NB] = jnp.where(fresh[k][:NB] & (first == 0), top, 0.0).astype(BF)
    stores = [pltpu.make_async_copy(share.at[0], share_hbm.at[0], sems.at[0])]
    stores[0].start()
    for k in range(0, STEPS, 2):
        at = k * NB
        row = jnp.dot(hot[at:at + 2 * NB, :], matrix[...], preferred_element_type=F32)
        for i in range(2):
            for c in range(0, width, NB):
                here = slice(at + i * NB, at + (i + 1) * NB)
                new = jnp.where(fresh[k + i][NB:], row[i * NB:(i + 1) * NB, c:c + NB], 0.0)
                share[1, here, c:c + NB] = new.astype(BF)
        both = pl.ds(at, 2 * NB)
        stores.append(pltpu.make_async_copy(share.at[1, both], share_hbm.at[1, both], sems.at[1 + k // 2]))
        stores[-1].start()
    for store in stores:
        store.wait()


def select_kernel(rows_ref, select_ref):
    for k in range(1, STEPS):
        for j, (last, live) in enumerate(last_match(matches(k, rows_ref)[1])[0]):
            at = start_of(k) + 2 * NB * j
            select_ref[:, at:at + NB] = last.astype(BF)
            select_ref[:, at + NB:at + 2 * NB] = (-live).astype(BF)


def mark_kernel(first_ref, rows_ref, matrix_ref, last_ref, live_ref, kept_ref):
    height = matrix_ref.shape[0]
    ids = iota((height, NB), 0) + first_ref[0] + pl.program_id(0) * height
    is_top = ids < TOP
    same = [jnp.where((ids == rows_ref[j:j + 1, :]) & ~is_top, 1.0, 0.0).astype(F32) for j in range(STEPS)]
    state, fresh = last_match(same)
    for j, (last, live) in enumerate(state):
        last_ref[:, NB * j:NB * (j + 1)] = last.astype(BF)
        live_ref[:, NB * j:NB * (j + 1)] = jnp.where(is_top, 0.0, -live).astype(BF)
    fresh = fresh & ~is_top
    for c in range(0, matrix_ref.shape[1], NB):
        kept_ref[:, c:c + NB] = jnp.where(fresh, matrix_ref[:, c:c + NB].astype(F32), 0.0).astype(BF)


def rows_kernel(first_ref, panels_ref, live_ref, lower_ref):
    height = 2 * NB

    def one(step, carry):
        at = pl.multiple_of(step * height, height)
        block = pl.ds(at, height)
        ids = iota((height, NB), 0) + first_ref[0] + at
        for j in range(STEPS):
            here = slice(NB * j, NB * (j + 1))
            diag = jnp.where((ids - NB * j == iota((height, NB), 1)) & (ids < TOP), 1.0, 0.0).astype(BF)
            lower_ref[block, here] = live_ref[block, here] * panels_ref[j, block, :] + diag
        return carry

    lax.fori_loop(0, panels_ref.shape[1] // height, one, 0)


def solve_kernel(core_ref, content_hbm, mine_hbm, other_hbm, inverses_hbm, select_hbm, last_hbm, lower_hbm, kept_hbm, out_hbm,
                 content, low, inverses, parts, coef, last, lower, kept, state, moved, upper, out, sems, out_sems):
    core = core_ref[0]
    height = out.shape[0] // BLOCKS
    copies = [
        pltpu.make_async_copy(src, dst, sems.at[i])
        for i, (src, dst) in enumerate((
            (inverses_hbm, inverses),
            (content_hbm, content),
            (mine_hbm, low.at[core]),
            (other_hbm, low.at[1 - core]),
            (select_hbm, coef),
            (last_hbm, last),
            (lower_hbm, lower),
            (kept_hbm, kept),
        ))
    ]
    for copy in copies:
        copy.start()
    copies[0].wait()
    for k in range(STEPS):
        rest = inverses[k]
        for i in range(3):
            parts[k, i * NB:(i + 1) * NB, :] = rest.astype(BF)
            rest = rest - rest.astype(BF).astype(F32)
    copies[1].wait()
    each = CHUNK
    for k in range(STEPS):
        x = content[:, k * NB:(k + 1) * NB, :].reshape(2 * NB, -1).astype(F32)
        if k == 1:
            for copy in copies[2:5]:
                copy.wait()
        if k:
            for j in range(k):
                at = start_of(k) + 2 * NB * j + NB
                for side in range(2):
                    for r in range(0, NB, each):
                        row = (2 * PAIRS.index((k, j)) + 1 - side) * NB + r
                        held, inside = divmod(row // each, low.shape[1])
                        here = side * NB + r
                        coef[here:here + each, at:at + NB] = coef[here:here + each, at:at + NB] * low[held, inside]
            at = start_of(k)
            x = x + jnp.dot(coef[:, at:at + 2 * NB * k], state[:2 * NB * k, :], preferred_element_type=F32)
        y = x.astype(BF)
        state[2 * NB * k:2 * NB * k + NB, :] = y[:NB]
        moved[k * NB:(k + 1) * NB, :] = y[:NB]
        u = jnp.dot(parts[k], y[NB:], preferred_element_type=F32)
        u = (u[:NB] + (u[NB:2 * NB] + u[2 * NB:])).astype(BF)
        state[2 * NB * k + NB:2 * NB * (k + 1), :] = u
        upper[k * NB:(k + 1) * NB, :] = u
    for copy in copies[5:]:
        copy.wait()
    writes = []
    for b in range(BLOCKS):
        at = b * height
        new = jnp.dot(last[at:at + height, :], moved[...], preferred_element_type=F32)
        new = new + jnp.dot(lower[at:at + height, :], upper[...], preferred_element_type=F32)
        out[at:at + height, :] = (kept[at:at + height, :].astype(F32) + new).astype(BF)
        writes.append(pltpu.make_async_copy(out.at[at:at + height], out_hbm.at[at:at + height], out_sems.at[b]))
        writes[-1].start()
    for write in writes:
        write.wait()


def cost(flops, nbytes):
    return pl.CostEstimate(flops=flops, bytes_accessed=nbytes, transcendentals=0)


def spread(x, axes, parts):
    return lax.all_to_all(jnp.broadcast_to(x[None], (parts,) + x.shape), axes, 0, 0, tiled=True)


def per_device(ny, nz, nx, nc, matrix, panels, inverses, pivots):
    nzx = nz * nx
    local, width = matrix.shape
    held = panels.shape[1]
    y, core = lax.axis_index("y"), lax.axis_index("c")
    z, x = lax.axis_index("z"), lax.axis_index("x")
    first = y * local
    swap = [(0, 1), (1, 0)]
    first1 = first.reshape(1).astype(jnp.int32)
    core1 = core.reshape(1).astype(jnp.int32)

    share = pl.pallas_call(
        share_kernel,
        out_shape=jax.ShapeDtypeStruct((2, TOP, width), BF),
        in_specs=[SM, VM, ANY],
        out_specs=ANY,
        scratch_shapes=[
            pltpu.VMEM((local, width), BF),
            pltpu.VMEM((TOP, local), BF),
            pltpu.VMEM((2, TOP, width), BF),
            pltpu.SemaphoreType.DMA((4,)),
        ],
        cost_estimate=cost(2 * TOP * local * width, 4 << 20),
    )(first1, pivots, matrix)
    content = lax.psum(share, "y")
    panels, pivots, _ = lax.optimization_barrier((panels, pivots, share))

    def gather(panels, pivots):
        column = spread(panels.reshape(STEPS * held, NB), "z", nz).reshape(nz, STEPS * held, NB)

        idx = []
        for k, j in PAIRS:
            for rows in (pivots[k], k * NB + jnp.arange(NB, dtype=jnp.int32)):
                here = rows - first
                pb = here // held
                at = (pb // (nx * nc) * STEPS + j) * held + here % held
                owned = (here >= 0) & (here < local) & (pb % (nx * nc) == x * nc + core)
                idx.append(jnp.where(owned, at, -1))
        chunk = -(-len(idx) * NB // (nzx * nc) // CHUNK) * CHUNK
        idx = jnp.concatenate(idx + [jnp.full((chunk * nzx * nc - len(idx) * NB,), -1, jnp.int32)])
        idx = lax.dynamic_slice(idx.reshape(nc, nz, nx * chunk), (0, z, 0), (nc, 1, nx * chunk)).reshape(nc * nx * chunk)
        part = jnp.take(column.reshape(-1, NB), jnp.maximum(idx, 0), axis=0)
        part = jnp.where((idx >= 0)[:, None], part, jnp.zeros((), BF)).reshape(nc * nx, chunk, NB)
        part = lax.all_to_all(part, ("c", "x"), 0, 0, tiled=True)
        part = part.astype(F32).sum(0).astype(BF)
        part, pivots, late = lax.optimization_barrier((part, pivots, column))
        part = spread(part, "y", ny)
        marked = pl.pallas_call(
            mark_kernel,
            out_shape=(jax.ShapeDtypeStruct((local, TOP), BF), jax.ShapeDtypeStruct((local, TOP), BF), jax.ShapeDtypeStruct((local, width), BF)),
            grid=(local // (2 * NB),),
            in_specs=[SM, pl.BlockSpec((STEPS, NB), lambda i: (0, 0)), pl.BlockSpec((2 * NB, width), lambda i: (i, 0))],
            out_specs=tuple(pl.BlockSpec((2 * NB, n), lambda i: (i, 0)) for n in (TOP, TOP, width)),
            cost_estimate=cost(4 * TOP * local * NB, 6 << 20),
        )(first1, pivots, matrix)
        part, *marked = lax.optimization_barrier((part, *marked))
        part = part.reshape(ny, chunk, NB).astype(F32).sum(0).astype(BF)

        blocks = [column] + [
            lax.ppermute(late if s % 2 else column, "x", [((i + s) % nx, i) for i in range(nx)]) for s in range(1, nx)
        ]
        mine = lax.dynamic_slice_in_dim(jnp.stack(blocks + blocks), (nx - x) % nx, nx)
        part = jnp.broadcast_to(part[None], (nzx, chunk, NB))
        part, mine, pivots = lax.optimization_barrier((part, mine, pivots))
        other = lax.ppermute(mine, "c", swap)
        select = pl.pallas_call(
            select_kernel,
            out_shape=jax.ShapeDtypeStruct((2 * NB, start_of(STEPS)), BF),
            in_specs=[VM],
            out_specs=VM,
            cost_estimate=cost(LONG, 2 << 20),
        )(pivots)
        other, select = lax.optimization_barrier((other, select))
        low_mine = lax.all_to_all(part, ("z", "x"), 0, 0, tiled=True)

        both = [a.reshape(nx, nz, STEPS, held, NB) for a in (mine, other)]
        both = jnp.stack([jnp.where(core == 0, both[0], both[1]), jnp.where(core == 0, both[1], both[0])])
        full = both.transpose(3, 2, 1, 0, 4, 5).reshape(STEPS, local, NB)
        lower = pl.pallas_call(
            rows_kernel,
            out_shape=jax.ShapeDtypeStruct((local, TOP), BF),
            in_specs=[SM, VM, VM],
            out_specs=VM,
            cost_estimate=cost(2 * TOP * local * NB, 12 << 20),
        )(first1, full, marked[1])
        low_mine, lower = lax.optimization_barrier((low_mine, lower))
        return low_mine, lax.ppermute(low_mine, "c", swap), marked[0], lower, marked[2], select

    def nothing(panels, pivots):
        return tuple(jnp.zeros(o.shape, o.dtype) for o in jax.eval_shape(gather, panels, pivots))

    low_mine, low_other, last, lower, kept, select = lax.cond(y < ny, gather, nothing, panels, pivots)

    chunk = low_mine.size // (nzx * NB)
    low_shape = (nzx * chunk // CHUNK, CHUNK, NB)
    return pl.pallas_call(
        solve_kernel,
        out_shape=jax.ShapeDtypeStruct((local, width), BF),
        in_specs=[SM] + [ANY] * 8,
        out_specs=ANY,
        scratch_shapes=[
            pltpu.VMEM((2, TOP, width), BF),
            pltpu.VMEM((2,) + low_shape, BF),
            pltpu.VMEM(inverses.shape, F32),
            pltpu.VMEM((STEPS, 3 * NB, NB), BF),
            pltpu.VMEM(select.shape, BF),
            pltpu.VMEM(last.shape, BF),
            pltpu.VMEM(lower.shape, BF),
            pltpu.VMEM((local, width), BF),
            pltpu.VMEM((2 * TOP, width), BF),
            pltpu.VMEM((TOP, width), BF),
            pltpu.VMEM((TOP, width), BF),
            pltpu.VMEM((local, width), BF),
            pltpu.SemaphoreType.DMA((8,)),
            pltpu.SemaphoreType.DMA((BLOCKS,)),
        ],
        cost_estimate=cost(4 * TOP * local * width, 16 << 20),
    )(core1, content, low_mine.reshape(low_shape), low_other.reshape(low_shape), inverses, select, last, lower, kept)


def solution(mesh):
    ny, npb = mesh.devices.shape
    nz, nx, nc = (8, 4, 2) if npb == 64 else (1, npb // 2, 2)
    fine = Mesh(mesh.devices.reshape(ny, nz, nx, nc), ("y", "z", "x", "c"))
    cols = ("z", "x", "c")
    in_specs = (P("y", cols), P(None, ("y",) + cols, None), P(), P())
    return jax.shard_map(
        functools.partial(per_device, ny, nz, nx, nc), mesh=fine, in_specs=in_specs, out_specs=P("y", cols), check_vma=False
    )
```

```python
import functools

import jax
import jax.numpy as jnp
from jax import lax
from jax.experimental import pallas as pl
from jax.experimental.pallas import tpu as pltpu
from jax.sharding import Mesh
from jax.sharding import PartitionSpec as P

NB = 128
STEPS = 6
TOP = NB * STEPS
PAIRS = [(k, j) for k in range(1, STEPS) for j in range(k)]
CHUNK = 64
BLOCKS = 3
LONG = 1 << 36
BF = jnp.bfloat16
F32 = jnp.float32
VM = pl.BlockSpec(memory_space=pltpu.VMEM)
SM = pl.BlockSpec(memory_space=pltpu.SMEM)
ANY = pl.BlockSpec(memory_space=pl.ANY)


def start_of(k):
    return 2 * NB * (k * (k - 1) // 2)


def iota(shape, dim):
    return lax.broadcasted_iota(jnp.int32, shape, dim)


def columns(row):
    return jnp.broadcast_to(row.astype(F32), (NB, NB)).T.astype(jnp.int32)


def matches(k, rows_ref):
    ids = jnp.concatenate([iota((NB, NB), 0) + k * NB, columns(rows_ref[k:k + 1, :])])
    return ids, [jnp.where(ids == rows_ref[j:j + 1, :], 1.0, 0.0).astype(F32) for j in range(k)]


def any_lane(same):
    return jnp.dot(same.astype(BF), jnp.ones((NB, NB), BF), preferred_element_type=F32)


def last_match(same):
    hits = [any_lane(s) for s in same]
    found = jnp.zeros(same[0].shape, F32)
    out = []
    for s, hit in zip(reversed(same), reversed(hits)):
        live = 1.0 - found
        out.append((s * live, live))
        found = jnp.maximum(found, hit)
    return out[::-1], found < 0.5


def share_kernel(first_ref, rows_ref, matrix_hbm, share_hbm, matrix, hot, share, sems):
    load = pltpu.make_async_copy(matrix_hbm, matrix, sems.at[0])
    load.start()
    first = first_ref[0]
    local, width = matrix.shape
    fresh = []
    for k in range(STEPS):
        ids, same = matches(k, rows_ref)
        fresh.append(any_lane(sum(same, jnp.zeros((2 * NB, NB), F32))) < 0.5)
        at = k * NB
        where = ids[NB:] - first
        for c in range(0, local, NB):
            hot[at:at + NB, c:c + NB] = jnp.where(iota((NB, NB), 1) + c == where, 1.0, 0.0).astype(BF)
    load.wait()
    for k in range(STEPS):
        at = k * NB
        for c in range(0, width, NB):
            top = matrix[at:at + NB, c:c + NB].astype(F32)
            share[0, at:at + NB, c:c + NB] = jnp.where(fresh[k][:NB] & (first == 0), top, 0.0).astype(BF)
    stores = [pltpu.make_async_copy(share.at[0], share_hbm.at[0], sems.at[0])]
    stores[0].start()
    for k in range(0, STEPS, 2):
        at = k * NB
        row = jnp.dot(hot[at:at + 2 * NB, :], matrix[...], preferred_element_type=F32)
        for i in range(2):
            for c in range(0, width, NB):
                here = slice(at + i * NB, at + (i + 1) * NB)
                new = jnp.where(fresh[k + i][NB:], row[i * NB:(i + 1) * NB, c:c + NB], 0.0)
                share[1, here, c:c + NB] = new.astype(BF)
        both = pl.ds(at, 2 * NB)
        stores.append(pltpu.make_async_copy(share.at[1, both], share_hbm.at[1, both], sems.at[1 + k // 2]))
        stores[-1].start()
    for store in stores:
        store.wait()


def select_kernel(rows_ref, select_ref):
    for k in range(1, STEPS):
        for j, (last, live) in enumerate(last_match(matches(k, rows_ref)[1])[0]):
            at = start_of(k) + 2 * NB * j
            select_ref[:, at:at + NB] = last.astype(BF)
            select_ref[:, at + NB:at + 2 * NB] = (-live).astype(BF)


def mark_kernel(first_ref, rows_ref, matrix_ref, last_ref, live_ref, kept_ref):
    height = 2 * NB

    def one(step, carry):
        at = pl.multiple_of(step * height, height)
        ids = iota((height, NB), 0) + first_ref[0] + at
        is_top = ids < TOP
        same = [jnp.where((ids == rows_ref[j:j + 1, :]) & ~is_top, 1.0, 0.0).astype(F32) for j in range(STEPS)]
        state, fresh = last_match(same)
        for j, (last, live) in enumerate(state):
            last_ref[pl.ds(at, height), NB * j:NB * (j + 1)] = last.astype(BF)
            live_ref[pl.ds(at, height), NB * j:NB * (j + 1)] = jnp.where(is_top, 0.0, -live).astype(BF)
        fresh = fresh & ~is_top
        for c in range(0, matrix_ref.shape[1], NB):
            old = matrix_ref[pl.ds(at, height), c:c + NB].astype(F32)
            kept_ref[pl.ds(at, height), c:c + NB] = jnp.where(fresh, old, 0.0).astype(BF)
        return carry

    lax.fori_loop(0, matrix_ref.shape[0] // height, one, 0)


def rows_kernel(first_ref, panels_ref, live_ref, lower_ref):
    height = 2 * NB

    def one(step, carry):
        at = pl.multiple_of(step * height, height)
        block = pl.ds(at, height)
        ids = iota((height, NB), 0) + first_ref[0] + at
        for j in range(STEPS):
            here = slice(NB * j, NB * (j + 1))
            diag = jnp.where((ids - NB * j == iota((height, NB), 1)) & (ids < TOP), 1.0, 0.0).astype(BF)
            lower_ref[block, here] = live_ref[block, here] * panels_ref[j, block, :] + diag
        return carry

    lax.fori_loop(0, panels_ref.shape[1] // height, one, 0)


def solve_kernel(core_ref, content_hbm, mine_hbm, other_hbm, inverses_hbm, select_hbm, last_hbm, lower_hbm, kept_hbm, out_hbm,
                 content, low, inverses, parts, coef, factor, kept, state, final, out, sems, out_sems):
    core = core_ref[0]
    height = out.shape[0] // BLOCKS
    copies = [
        pltpu.make_async_copy(src, dst, sems.at[i])
        for i, (src, dst) in enumerate((
            (inverses_hbm, inverses),
            (content_hbm, content),
            (mine_hbm, low.at[core]),
            (other_hbm, low.at[1 - core]),
            (select_hbm, coef),
            (last_hbm, factor.at[:, :TOP]),
            (lower_hbm, factor.at[:, TOP:]),
            (kept_hbm, kept),
        ))
    ]
    for copy in copies:
        copy.start()
    copies[0].wait()
    for k in range(STEPS):
        rest = inverses[k]
        for i in range(3):
            parts[k, i * NB:(i + 1) * NB, :] = rest.astype(BF)
            rest = rest - rest.astype(BF).astype(F32)
    copies[1].wait()
    each = CHUNK
    for k in range(STEPS):
        x = content[:, k * NB:(k + 1) * NB, :].reshape(2 * NB, -1).astype(F32)
        if k == 1:
            for copy in copies[2:5]:
                copy.wait()
        if k:
            for j in range(k):
                at = start_of(k) + 2 * NB * j + NB
                for side in range(2):
                    for r in range(0, NB, each):
                        row = (2 * PAIRS.index((k, j)) + 1 - side) * NB + r
                        held, inside = divmod(row // each, low.shape[1])
                        here = side * NB + r
                        coef[here:here + each, at:at + NB] = coef[here:here + each, at:at + NB] * low[held, inside]
            at = start_of(k)
            x = x + jnp.dot(coef[:, at:at + 2 * NB * k], state[:2 * NB * k, :], preferred_element_type=F32)
        y = x.astype(BF)
        state[2 * NB * k:2 * NB * k + NB, :] = y[:NB]
        final[k * NB:(k + 1) * NB, :] = y[:NB]
        u = jnp.dot(parts[k], y[NB:], preferred_element_type=F32)
        u = (u[:NB] + (u[NB:2 * NB] + u[2 * NB:])).astype(BF)
        state[2 * NB * k + NB:2 * NB * (k + 1), :] = u
        final[TOP + k * NB:TOP + (k + 1) * NB, :] = u
    for copy in copies[5:]:
        copy.wait()
    writes = []
    for b in range(BLOCKS):
        at = b * height
        new = jnp.dot(factor[at:at + height, :], final[...], preferred_element_type=F32)
        out[at:at + height, :] = (kept[at:at + height, :].astype(F32) + new).astype(BF)
        writes.append(pltpu.make_async_copy(out.at[at:at + height], out_hbm.at[at:at + height], out_sems.at[b]))
        writes[-1].start()
    for write in writes:
        write.wait()


def cost(flops, nbytes):
    return pl.CostEstimate(flops=flops, bytes_accessed=nbytes, transcendentals=0)


def spread(x, axes, parts):
    return lax.all_to_all(jnp.broadcast_to(x[None], (parts,) + x.shape), axes, 0, 0, tiled=True)


def per_device(ny, nz, nx, nc, matrix, panels, inverses, pivots):
    nzx = nz * nx
    local, width = matrix.shape
    held = panels.shape[1]
    y, core = lax.axis_index("y"), lax.axis_index("c")
    z, x = lax.axis_index("z"), lax.axis_index("x")
    first = y * local
    swap = [(0, 1), (1, 0)]
    first1 = first.reshape(1).astype(jnp.int32)
    core1 = core.reshape(1).astype(jnp.int32)

    share = pl.pallas_call(
        share_kernel,
        out_shape=jax.ShapeDtypeStruct((2, TOP, width), BF),
        in_specs=[SM, VM, ANY],
        out_specs=ANY,
        scratch_shapes=[
            pltpu.VMEM((local, width), BF),
            pltpu.VMEM((TOP, local), BF),
            pltpu.VMEM((2, TOP, width), BF),
            pltpu.SemaphoreType.DMA((4,)),
        ],
        cost_estimate=cost(2 * TOP * local * width, 4 << 20),
    )(first1, pivots, matrix)
    content = lax.psum(share, "y")
    panels, pivots, _ = lax.optimization_barrier((panels, pivots, share))

    def gather(panels, pivots):
        column = spread(panels.reshape(STEPS * held, NB), "z", nz).reshape(nz, STEPS * held, NB)

        idx = []
        for k, j in PAIRS:
            for rows in (pivots[k], k * NB + jnp.arange(NB, dtype=jnp.int32)):
                here = rows - first
                pb = here // held
                at = (pb // (nx * nc) * STEPS + j) * held + here % held
                owned = (here >= 0) & (here < local) & (pb % (nx * nc) == x * nc + core)
                idx.append(jnp.where(owned, at, -1))
        chunk = -(-len(idx) * NB // (nzx * nc) // CHUNK) * CHUNK
        idx = jnp.concatenate(idx + [jnp.full((chunk * nzx * nc - len(idx) * NB,), -1, jnp.int32)])
        idx = lax.dynamic_slice(idx.reshape(nc, nz, nx * chunk), (0, z, 0), (nc, 1, nx * chunk)).reshape(nc * nx * chunk)
        part = jnp.take(column.reshape(-1, NB), jnp.maximum(idx, 0), axis=0)
        part = jnp.where((idx >= 0)[:, None], part, jnp.zeros((), BF)).reshape(nc * nx, chunk, NB)
        part = lax.all_to_all(part, ("c", "x"), 0, 0, tiled=True)
        part = part.astype(F32).sum(0).astype(BF)
        part, pivots = lax.optimization_barrier((part, pivots))
        part = spread(part, "y", ny)
        marked = pl.pallas_call(
            mark_kernel,
            out_shape=(jax.ShapeDtypeStruct((local, TOP), BF), jax.ShapeDtypeStruct((local, TOP), BF), jax.ShapeDtypeStruct((local, width), BF)),
            in_specs=[SM, VM, VM],
            out_specs=(VM, VM, VM),
            cost_estimate=cost(4 * TOP * local * NB, 6 << 20),
        )(first1, pivots, matrix)
        part, *marked = lax.optimization_barrier((part, *marked))
        part = part.reshape(ny, chunk, NB).astype(F32).sum(0).astype(BF)

        blocks = [column] + [lax.ppermute(column, "x", [((i + s) % nx, i) for i in range(nx)]) for s in range(1, nx)]
        mine = lax.dynamic_slice_in_dim(jnp.stack(blocks + blocks), (nx - x) % nx, nx)
        part = jnp.broadcast_to(part[None], (nzx, chunk, NB))
        part, mine, pivots = lax.optimization_barrier((part, mine, pivots))
        other = lax.ppermute(mine, "c", swap)
        select = pl.pallas_call(
            select_kernel,
            out_shape=jax.ShapeDtypeStruct((2 * NB, start_of(STEPS)), BF),
            in_specs=[VM],
            out_specs=VM,
            cost_estimate=cost(LONG, 2 << 20),
        )(pivots)
        other, select = lax.optimization_barrier((other, select))
        low_mine = lax.all_to_all(part, ("z", "x"), 0, 0, tiled=True)

        both = [a.reshape(nx, nz, STEPS, held, NB) for a in (mine, other)]
        both = jnp.stack([jnp.where(core == 0, both[0], both[1]), jnp.where(core == 0, both[1], both[0])])
        full = both.transpose(3, 2, 1, 0, 4, 5).reshape(STEPS, local, NB)
        lower = pl.pallas_call(
            rows_kernel,
            out_shape=jax.ShapeDtypeStruct((local, TOP), BF),
            in_specs=[SM, VM, VM],
            out_specs=VM,
            cost_estimate=cost(2 * TOP * local * NB, 12 << 20),
        )(first1, full, marked[1])
        low_mine, lower = lax.optimization_barrier((low_mine, lower))
        return low_mine, lax.ppermute(low_mine, "c", swap), marked[0], lower, marked[2], select

    def nothing(panels, pivots):
        return tuple(jnp.zeros(o.shape, o.dtype) for o in jax.eval_shape(gather, panels, pivots))

    low_mine, low_other, last, lower, kept, select = lax.cond(y < ny, gather, nothing, panels, pivots)

    chunk = low_mine.size // (nzx * NB)
    low_shape = (nzx * chunk // CHUNK, CHUNK, NB)
    return pl.pallas_call(
        solve_kernel,
        out_shape=jax.ShapeDtypeStruct((local, width), BF),
        in_specs=[SM] + [ANY] * 8,
        out_specs=ANY,
        scratch_shapes=[
            pltpu.VMEM((2, TOP, width), BF),
            pltpu.VMEM((2,) + low_shape, BF),
            pltpu.VMEM(inverses.shape, F32),
            pltpu.VMEM((STEPS, 3 * NB, NB), BF),
            pltpu.VMEM(select.shape, BF),
            pltpu.VMEM((local, 2 * TOP), BF),
            pltpu.VMEM((local, width), BF),
            pltpu.VMEM((2 * TOP, width), BF),
            pltpu.VMEM((2 * TOP, width), BF),
            pltpu.VMEM((local, width), BF),
            pltpu.SemaphoreType.DMA((8,)),
            pltpu.SemaphoreType.DMA((BLOCKS,)),
        ],
        cost_estimate=cost(4 * TOP * local * width, 16 << 20),
    )(core1, content, low_mine.reshape(low_shape), low_other.reshape(low_shape), inverses, select, last, lower, kept)


def solution(mesh):
    ny, npb = mesh.devices.shape
    nz, nx, nc = (8, 4, 2) if npb == 64 else (1, npb // 2, 2)
    fine = Mesh(mesh.devices.reshape(ny, nz, nx, nc), ("y", "z", "x", "c"))
    cols = ("z", "x", "c")
    in_specs = (P("y", cols), P(None, ("y",) + cols, None), P(), P())
    return jax.shard_map(
        functools.partial(per_device, ny, nz, nx, nc), mesh=fine, in_specs=in_specs, out_specs=P("y", cols), check_vma=False
    )
```

```python
import functools

import jax
import jax.numpy as jnp
from jax import lax
from jax.experimental import pallas as pl
from jax.experimental.pallas import tpu as pltpu
from jax.sharding import Mesh
from jax.sharding import PartitionSpec as P

NB = 128
STEPS = 6
TOP = NB * STEPS
PAIRS = [(k, j) for k in range(1, STEPS) for j in range(k)]
CHUNK = 64
BLOCKS = 3
LONG = 1 << 36
BF = jnp.bfloat16
F32 = jnp.float32
VM = pl.BlockSpec(memory_space=pltpu.VMEM)
SM = pl.BlockSpec(memory_space=pltpu.SMEM)
ANY = pl.BlockSpec(memory_space=pl.ANY)


def start_of(k):
    return 2 * NB * (k * (k - 1) // 2)


def iota(shape, dim):
    return lax.broadcasted_iota(jnp.int32, shape, dim)


def columns(row):
    return jnp.broadcast_to(row.astype(F32), (NB, NB)).T.astype(jnp.int32)


def matches(k, rows_ref):
    ids = jnp.concatenate([iota((NB, NB), 0) + k * NB, columns(rows_ref[k:k + 1, :])])
    return ids, [jnp.where(ids == rows_ref[j:j + 1, :], 1.0, 0.0).astype(F32) for j in range(k)]


def any_lane(same):
    return jnp.dot(same.astype(BF), jnp.ones((NB, NB), BF), preferred_element_type=F32)


def last_match(same):
    hits = [any_lane(s) for s in same]
    found = jnp.zeros(same[0].shape, F32)
    out = []
    for s, hit in zip(reversed(same), reversed(hits)):
        live = 1.0 - found
        out.append((s * live, live))
        found = jnp.maximum(found, hit)
    return out[::-1], found < 0.5


def share_kernel(first_ref, rows_ref, matrix_hbm, share_hbm, matrix, hot, share, sems):
    load = pltpu.make_async_copy(matrix_hbm, matrix, sems.at[0])
    load.start()
    first = first_ref[0]
    local, width = matrix.shape
    fresh = []
    for k in range(STEPS):
        ids, same = matches(k, rows_ref)
        fresh.append(any_lane(sum(same, jnp.zeros((2 * NB, NB), F32))) < 0.5)
        at = k * NB
        where = ids[NB:] - first
        for c in range(0, local, NB):
            hot[at:at + NB, c:c + NB] = jnp.where(iota((NB, NB), 1) + c == where, 1.0, 0.0).astype(BF)
    load.wait()
    for k in range(STEPS):
        at = k * NB
        for c in range(0, width, NB):
            top = matrix[at:at + NB, c:c + NB].astype(F32)
            share[0, at:at + NB, c:c + NB] = jnp.where(fresh[k][:NB] & (first == 0), top, 0.0).astype(BF)
    stores = [pltpu.make_async_copy(share.at[0], share_hbm.at[0], sems.at[0])]
    stores[0].start()
    for k in range(0, STEPS, 2):
        at = k * NB
        row = jnp.dot(hot[at:at + 2 * NB, :], matrix[...], preferred_element_type=F32)
        for i in range(2):
            for c in range(0, width, NB):
                here = slice(at + i * NB, at + (i + 1) * NB)
                new = jnp.where(fresh[k + i][NB:], row[i * NB:(i + 1) * NB, c:c + NB], 0.0)
                share[1, here, c:c + NB] = new.astype(BF)
        both = pl.ds(at, 2 * NB)
        stores.append(pltpu.make_async_copy(share.at[1, both], share_hbm.at[1, both], sems.at[1 + k // 2]))
        stores[-1].start()
    for store in stores:
        store.wait()


def select_kernel(rows_ref, select_ref):
    for k in range(1, STEPS):
        for j, (last, live) in enumerate(last_match(matches(k, rows_ref)[1])[0]):
            at = start_of(k) + 2 * NB * j
            select_ref[:, at:at + NB] = last.astype(BF)
            select_ref[:, at + NB:at + 2 * NB] = (-live).astype(BF)


def mark_kernel(first_ref, rows_ref, matrix_ref, last_ref, live_ref, kept_ref):
    height = 2 * NB

    def one(step, carry):
        at = pl.multiple_of(step * height, height)
        ids = iota((height, NB), 0) + first_ref[0] + at
        is_top = ids < TOP
        same = [jnp.where((ids == rows_ref[j:j + 1, :]) & ~is_top, 1.0, 0.0).astype(F32) for j in range(STEPS)]
        state, fresh = last_match(same)
        for j, (last, live) in enumerate(state):
            last_ref[pl.ds(at, height), NB * j:NB * (j + 1)] = last.astype(BF)
            live_ref[pl.ds(at, height), NB * j:NB * (j + 1)] = jnp.where(is_top, 0.0, -live).astype(BF)
        fresh = fresh & ~is_top
        for c in range(0, matrix_ref.shape[1], NB):
            old = matrix_ref[pl.ds(at, height), c:c + NB].astype(F32)
            kept_ref[pl.ds(at, height), c:c + NB] = jnp.where(fresh, old, 0.0).astype(BF)
        return carry

    lax.fori_loop(0, matrix_ref.shape[0] // height, one, 0)


def rows_kernel(first_ref, panels_ref, live_ref, lower_ref):
    height = 2 * NB

    def one(step, carry):
        at = pl.multiple_of(step * height, height)
        block = pl.ds(at, height)
        ids = iota((height, NB), 0) + first_ref[0] + at
        for j in range(STEPS):
            here = slice(NB * j, NB * (j + 1))
            diag = jnp.where((ids - NB * j == iota((height, NB), 1)) & (ids < TOP), 1.0, 0.0).astype(BF)
            lower_ref[block, here] = live_ref[block, here] * panels_ref[j, block, :] + diag
        return carry

    lax.fori_loop(0, panels_ref.shape[1] // height, one, 0)


def solve_kernel(core_ref, content_hbm, mine_hbm, other_hbm, inverses_hbm, select_hbm, last_hbm, lower_hbm, kept_hbm, out_hbm,
                 content, low, inverses, parts, coef, factor, kept, state, final, out, sems, out_sems):
    core = core_ref[0]
    height = out.shape[0] // BLOCKS
    copies = [
        pltpu.make_async_copy(src, dst, sems.at[i])
        for i, (src, dst) in enumerate((
            (inverses_hbm, inverses),
            (content_hbm, content),
            (mine_hbm, low.at[core]),
            (other_hbm, low.at[1 - core]),
            (select_hbm, coef),
            (last_hbm, factor.at[:, :TOP]),
            (lower_hbm, factor.at[:, TOP:]),
            (kept_hbm, kept),
        ))
    ]
    for copy in copies[:5]:
        copy.start()
    copies[0].wait()
    for k in range(STEPS):
        rest = inverses[k]
        for i in range(3):
            parts[k, i * NB:(i + 1) * NB, :] = rest.astype(BF)
            rest = rest - rest.astype(BF).astype(F32)
    copies[1].wait()
    for copy in copies[5:]:
        copy.start()
    each = CHUNK
    for k in range(STEPS):
        x = content[:, k * NB:(k + 1) * NB, :].reshape(2 * NB, -1).astype(F32)
        if k == 1:
            for copy in copies[2:5]:
                copy.wait()
        if k:
            for j in range(k):
                at = start_of(k) + 2 * NB * j + NB
                for side in range(2):
                    for r in range(0, NB, each):
                        row = (2 * PAIRS.index((k, j)) + 1 - side) * NB + r
                        held, inside = divmod(row // each, low.shape[1])
                        here = side * NB + r
                        coef[here:here + each, at:at + NB] = coef[here:here + each, at:at + NB] * low[held, inside]
            at = start_of(k)
            x = x + jnp.dot(coef[:, at:at + 2 * NB * k], state[:2 * NB * k, :], preferred_element_type=F32)
        y = x.astype(BF)
        state[2 * NB * k:2 * NB * k + NB, :] = y[:NB]
        final[k * NB:(k + 1) * NB, :] = y[:NB]
        u = jnp.dot(parts[k], y[NB:], preferred_element_type=F32)
        u = (u[:NB] + (u[NB:2 * NB] + u[2 * NB:])).astype(BF)
        state[2 * NB * k + NB:2 * NB * (k + 1), :] = u
        final[TOP + k * NB:TOP + (k + 1) * NB, :] = u
    for copy in copies[5:]:
        copy.wait()
    writes = []
    for b in range(BLOCKS):
        at = b * height
        new = jnp.dot(factor[at:at + height, :], final[...], preferred_element_type=F32)
        out[at:at + height, :] = (kept[at:at + height, :].astype(F32) + new).astype(BF)
        writes.append(pltpu.make_async_copy(out.at[at:at + height], out_hbm.at[at:at + height], out_sems.at[b]))
        writes[-1].start()
    for write in writes:
        write.wait()


def cost(flops, nbytes):
    return pl.CostEstimate(flops=flops, bytes_accessed=nbytes, transcendentals=0)


def spread(x, axes, parts):
    return lax.all_to_all(jnp.broadcast_to(x[None], (parts,) + x.shape), axes, 0, 0, tiled=True)


def per_device(ny, nz, nx, nc, matrix, panels, inverses, pivots):
    nzx = nz * nx
    local, width = matrix.shape
    held = panels.shape[1]
    y, core = lax.axis_index("y"), lax.axis_index("c")
    z, x = lax.axis_index("z"), lax.axis_index("x")
    first = y * local
    swap = [(0, 1), (1, 0)]
    first1 = first.reshape(1).astype(jnp.int32)
    core1 = core.reshape(1).astype(jnp.int32)

    share = pl.pallas_call(
        share_kernel,
        out_shape=jax.ShapeDtypeStruct((2, TOP, width), BF),
        in_specs=[SM, VM, ANY],
        out_specs=ANY,
        scratch_shapes=[
            pltpu.VMEM((local, width), BF),
            pltpu.VMEM((TOP, local), BF),
            pltpu.VMEM((2, TOP, width), BF),
            pltpu.SemaphoreType.DMA((4,)),
        ],
        cost_estimate=cost(2 * TOP * local * width, 4 << 20),
    )(first1, pivots, matrix)
    content = lax.psum(share, "y")
    panels, pivots, _ = lax.optimization_barrier((panels, pivots, share))

    def gather(panels, pivots):
        column = spread(panels.reshape(STEPS * held, NB), "z", nz).reshape(nz, STEPS * held, NB)

        idx = []
        for k, j in PAIRS:
            for rows in (pivots[k], k * NB + jnp.arange(NB, dtype=jnp.int32)):
                here = rows - first
                pb = here // held
                at = (pb // (nx * nc) * STEPS + j) * held + here % held
                owned = (here >= 0) & (here < local) & (pb % (nx * nc) == x * nc + core)
                idx.append(jnp.where(owned, at, -1))
        chunk = -(-len(idx) * NB // (nzx * nc) // CHUNK) * CHUNK
        idx = jnp.concatenate(idx + [jnp.full((chunk * nzx * nc - len(idx) * NB,), -1, jnp.int32)])
        idx = lax.dynamic_slice(idx.reshape(nc, nz, nx * chunk), (0, z, 0), (nc, 1, nx * chunk)).reshape(nc * nx * chunk)
        part = jnp.take(column.reshape(-1, NB), jnp.maximum(idx, 0), axis=0)
        part = jnp.where((idx >= 0)[:, None], part, jnp.zeros((), BF)).reshape(nc * nx, chunk, NB)
        part = lax.all_to_all(part, ("c", "x"), 0, 0, tiled=True)
        part = part.astype(F32).sum(0).astype(BF)
        part, pivots = lax.optimization_barrier((part, pivots))
        part = spread(part, "y", ny)
        marked = pl.pallas_call(
            mark_kernel,
            out_shape=(jax.ShapeDtypeStruct((local, TOP), BF), jax.ShapeDtypeStruct((local, TOP), BF), jax.ShapeDtypeStruct((local, width), BF)),
            in_specs=[SM, VM, VM],
            out_specs=(VM, VM, VM),
            cost_estimate=cost(4 * TOP * local * NB, 6 << 20),
        )(first1, pivots, matrix)
        part, *marked = lax.optimization_barrier((part, *marked))
        part = part.reshape(ny, chunk, NB).astype(F32).sum(0).astype(BF)

        blocks = [column] + [lax.ppermute(column, "x", [((i + s) % nx, i) for i in range(nx)]) for s in range(1, nx)]
        mine = lax.dynamic_slice_in_dim(jnp.stack(blocks + blocks), (nx - x) % nx, nx)
        part = jnp.broadcast_to(part[None], (nzx, chunk, NB))
        part, mine, pivots = lax.optimization_barrier((part, mine, pivots))
        other = lax.ppermute(mine, "c", swap)
        select = pl.pallas_call(
            select_kernel,
            out_shape=jax.ShapeDtypeStruct((2 * NB, start_of(STEPS)), BF),
            in_specs=[VM],
            out_specs=VM,
            cost_estimate=cost(LONG, 2 << 20),
        )(pivots)
        other, select = lax.optimization_barrier((other, select))
        low_mine = lax.all_to_all(part, ("z", "x"), 0, 0, tiled=True)

        both = [a.reshape(nx, nz, STEPS, held, NB) for a in (mine, other)]
        both = jnp.stack([jnp.where(core == 0, both[0], both[1]), jnp.where(core == 0, both[1], both[0])])
        full = both.transpose(3, 2, 1, 0, 4, 5).reshape(STEPS, local, NB)
        lower = pl.pallas_call(
            rows_kernel,
            out_shape=jax.ShapeDtypeStruct((local, TOP), BF),
            in_specs=[SM, VM, VM],
            out_specs=VM,
            cost_estimate=cost(2 * TOP * local * NB, 12 << 20),
        )(first1, full, marked[1])
        low_mine, lower = lax.optimization_barrier((low_mine, lower))
        return low_mine, lax.ppermute(low_mine, "c", swap), marked[0], lower, marked[2], select

    def nothing(panels, pivots):
        return tuple(jnp.zeros(o.shape, o.dtype) for o in jax.eval_shape(gather, panels, pivots))

    low_mine, low_other, last, lower, kept, select = lax.cond(y < ny, gather, nothing, panels, pivots)

    chunk = low_mine.size // (nzx * NB)
    low_shape = (nzx * chunk // CHUNK, CHUNK, NB)
    return pl.pallas_call(
        solve_kernel,
        out_shape=jax.ShapeDtypeStruct((local, width), BF),
        in_specs=[SM] + [ANY] * 8,
        out_specs=ANY,
        scratch_shapes=[
            pltpu.VMEM((2, TOP, width), BF),
            pltpu.VMEM((2,) + low_shape, BF),
            pltpu.VMEM(inverses.shape, F32),
            pltpu.VMEM((STEPS, 3 * NB, NB), BF),
            pltpu.VMEM(select.shape, BF),
            pltpu.VMEM((local, 2 * TOP), BF),
            pltpu.VMEM((local, width), BF),
            pltpu.VMEM((2 * TOP, width), BF),
            pltpu.VMEM((2 * TOP, width), BF),
            pltpu.VMEM((local, width), BF),
            pltpu.SemaphoreType.DMA((8,)),
            pltpu.SemaphoreType.DMA((BLOCKS,)),
        ],
        cost_estimate=cost(4 * TOP * local * width, 16 << 20),
    )(core1, content, low_mine.reshape(low_shape), low_other.reshape(low_shape), inverses, select, last, lower, kept)


def solution(mesh):
    ny, npb = mesh.devices.shape
    nz, nx, nc = (8, 4, 2) if npb == 64 else (1, npb // 2, 2)
    fine = Mesh(mesh.devices.reshape(ny, nz, nx, nc), ("y", "z", "x", "c"))
    cols = ("z", "x", "c")
    in_specs = (P("y", cols), P(None, ("y",) + cols, None), P(), P())
    return jax.shard_map(
        functools.partial(per_device, ny, nz, nx, nc), mesh=fine, in_specs=in_specs, out_specs=P("y", cols), check_vma=False
    )
```
